256 devices in a mesh: shard: 64 (over z, y, core), help: 4 (over x).
Axes of the slice: x: 4, y: 4, z: 8, core: 2. Of those that a mesh axis runs over, the one named last changes fastest.
Arguments:
- queries: bfloat16 [65536, 768], P(('shard', 'help')), may hold values from -6 to 6
- probe_group: int32 [65536, 2], P(('shard', 'help')), may hold values from 0 to 63, all different within a row; in each aligned block of 256 rows (0 to 255, 256 to 511, ...) at most 16 rows name the same one
- probe_local: int32 [65536, 2], P(('shard', 'help')), may hold values from 0 to 3
- points: bfloat16 [262144, 768], P(('shard', 'help')), may hold values from -6 to 6
- point_cluster: int32 [64, 4096], P('shard'), may hold values from 0 to 3, never falling along the last dimension, each value on 1 to 3072 neighbouring positions
- test_matrix: bfloat16 [32, 262144], P(None, ('shard', 'help')), may hold values from -6 to 6
Outputs:
- sketch: float32 [32, 262144], P(None, ('shard', 'help'))
- regressor: float32 [256, 32, 768], P(('shard', 'help'))
The draws below stay inside these ranges and needn't reach their ends.
Inputs may be any that keep to these rules, and one draw needn't show every extreme that they name: `probe_group`: A query's 2 groups differ. Among the 256 queries of one device (aligned blocks of rows), at most 16 pairs (q,k) name one group, and in some blocks one group is named exactly 16 times.
All inputs are finite; a program needn't handle non-finite values.
Results may differ from the reference program's by a relative error of at most 0.0037.
Values may be sent and summed in bfloat16 or wider, within the bound.
A program may use at most 64 MiB of HBM per device.

```python
import math
import jax
import jax.numpy as jnp
import numpy as np
from jax import lax

D = 768
R = 32
PROBES = 2
QDEV = 256
GROUPS = 64
GCL = 4
GPOINTS = 4096
CAP = 16
SEGMOST = 3072
QUERIES = 65536
POINTS = 262144


def with_ends(values, key, low, high):
    longest = values.shape.index(max(values.shape))
    spots = []
    for shift in (0, 1):
        where = [jax.random.randint(jax.random.fold_in(key, axis), (), 0, length) for axis, length in enumerate(values.shape)]
        where[longest] = (where[longest] + shift) % values.shape[longest]
        spots.append(tuple(where))
    return values.at[spots[0]].set(low).at[spots[1]].set(high)


def shard_levels(rng, extent, cuts, low, largest):
    def one(dim, parts):
        draws = jax.random.uniform(jax.random.fold_in(jax.random.fold_in(rng, 6), dim), (parts,), jnp.float32, low / len(cuts), largest / len(cuts))
        return jnp.repeat(jnp.exp(draws), extent[dim] // parts).reshape((-1,) + (1,) * (len(extent) - dim - 1))

    gain = one(*cuts[0])
    for cut in cuts[1:]:
        gain = gain * one(*cut)
    return gain


def rank_bounds(amount, slope):
    portions = [(1 << 20) // math.isqrt(grade ** slope) + 1 for grade in range(1, amount + 1)]
    spread = 1 + sum(portions) // (1 << 30)
    return np.cumsum(np.array([max(1, weight // spread) for weight in portions]))


def ranked(rng, dims, number_of, lean):
    listing = rank_bounds(number_of, lean)
    ticket = jax.random.randint(jax.random.fold_in(rng, 1), dims, 0, int(listing[number_of - 1]))
    standing = jnp.searchsorted(jnp.asarray(listing, jnp.int32), ticket, side="right")
    return jax.random.permutation(jax.random.fold_in(rng, 2), number_of)[standing].astype(jnp.int32)


def length_profile(amount, total, bound, lean):
    portions = [(1 << 20) // math.isqrt(standing ** lean) + 1 for standing in range(2, amount + 1)]
    surplus, counts = total - bound - (amount - 1), [1] * (amount - 1)
    while surplus > 0:
        candidates = [i for i in range(amount - 1) if counts[i] < bound]
        pool, remaining = sum([portions[i] for i in candidates]), surplus
        for i in candidates:
            more = min(bound - counts[i], max(1, remaining * portions[i] // pool), surplus)
            counts[i] = counts[i] + more
            surplus = surplus - more
    return np.array([bound] + counts)


def ragged(key, count, total, limit, lean):
    if count == 2:
        one = jax.random.randint(key, (), max(1, total - limit), min(limit, total - 1) + 1)
        return jnp.stack([one, total - one])
    lengths = jnp.asarray(length_profile(count, total, limit, lean), jnp.int32)
    twos = (count - 1) // 2
    source_of, sink = lengths[1:1 + 2 * twos:2], lengths[2:2 + 2 * twos:2]
    room = jnp.minimum(source_of - 1, limit - sink)
    passed = jax.random.randint(jax.random.fold_in(key, 1), (twos,), 0, 1 << 20) % (room + 1)
    lengths = lengths.at[1:1 + 2 * twos:2].set(source_of - passed).at[2:2 + 2 * twos:2].set(sink + passed)
    return lengths[jax.random.permutation(jax.random.fold_in(key, 2), count)]


def routed_block(key, own, number, rows, count, top, reach, slope):
    order = jax.random.permutation(key, count)
    heavy_load, usual = load_shares(count, rows * top, reach, slope, True), load_shares(count, rows * top, reach, slope, False)
    places = jnp.arange(count)

    def named(lengths, rotation):
        used = int((lengths > 0).sum())
        fixed = max(1, used // 4)
        moved = fixed + (places - fixed + rotation * (used - fixed)) % max(1, count - fixed)
        return jnp.zeros((count,), jnp.int32).at[order[jnp.where(places < fixed, places, moved)]].set(jnp.asarray(lengths, jnp.int32))

    lengths = jnp.where(number % 4 == 0, named(heavy_load, number // 4), named(usual, number - number // 4 - 1))
    mixed = jax.random.permutation(jax.random.fold_in(own, 3), count)
    donor, taker = mixed[0:count // 2 * 2:2], mixed[1:count // 2 * 2:2]
    slack = jnp.minimum(lengths[donor] - 1, reach - lengths[taker]) // 2
    slack = jnp.where((donor == order[0]) | (taker == order[0]) | (lengths[taker] == 0), 0, jnp.maximum(slack, 0))
    moved = jax.random.randint(jax.random.fold_in(own, 4), (count // 2,), 0, 1 << 20) % (slack + 1)
    lengths = lengths.at[donor].add(-moved).at[taker].add(moved)
    items = jnp.searchsorted(jnp.cumsum(lengths), jnp.arange(rows * top), side="right").astype(jnp.int32)
    grid = items.reshape(top, rows).T
    grid = grid[jax.random.permutation(jax.random.fold_in(own, 1), rows)]
    rotation = jax.random.randint(jax.random.fold_in(own, 2), (rows, 1), 0, top)
    return jnp.take_along_axis(grid, (jnp.arange(top)[None, :] + rotation) % top, axis=1)


def load_shares(count, total, most, skew, full):
    weights = [(1 << 20) // math.isqrt(grade ** skew) + 1 for grade in range(1, count + 1)]
    largest = most if full else min(most, max(-(-total // count), total * weights[0] // sum(weights)))
    least = 1 if total - largest >= count - 1 else 0
    given, surplus = [largest] + [least] * (count - 1), total - largest - least * (count - 1)
    while surplus > 0:
        candidates = [i for i in range(1, count) if given[i] < largest] or [i for i in range(1, count) if given[i] < most]
        mass, remaining = sum([weights[i] for i in candidates]), surplus
        for i in candidates:
            addition = min(most - given[i], max(1, remaining * weights[i] // mass), surplus)
            given[i] = given[i] + addition
            surplus = surplus - addition
    return np.array(given)


def centred(key, extent, scale, limit, split=(), kind=jnp.bfloat16):
    values = scale * jax.random.normal(key, extent, jnp.float32)
    if split:
        values = values * shard_levels(key, extent, split, -0.22, 0.18)
    return jnp.clip(values, -limit, limit).astype(kind)


def setup_inputs(seed: int = 0) -> dict:
    key_of = jax.random.split(jax.random.key(seed), 7)
    queries = centred(key_of[0], (QUERIES, D), 1.0, 6.0, ((0, 256),))
    probe_group_keys = jax.random.split(jax.random.fold_in(key_of[1], 1), QUERIES // QDEV)
    probe_group_turns = jax.random.permutation(jax.random.fold_in(key_of[1], 3), QUERIES // QDEV)
    probe_group = jax.vmap(lambda own, number: routed_block(jax.random.fold_in(key_of[1], 2), own, number, QDEV, GROUPS, PROBES, CAP, 2))(probe_group_keys, probe_group_turns).reshape((QUERIES, PROBES))
    probe_local = with_ends(ranked(key_of[2], (QUERIES, PROBES), GCL, 2), jax.random.fold_in(key_of[2], 3), 0, GCL - 1).astype(jnp.int32)
    points = centred(key_of[3], (POINTS, D), 1.0, 6.0, ((0, 256),))
    point_cluster = jax.vmap(lambda own: jnp.searchsorted(jnp.cumsum(ragged(own, GCL, GPOINTS, SEGMOST, 2)), jnp.arange(GPOINTS), side="right"))(jax.random.split(key_of[4], GROUPS)).reshape((GROUPS, GPOINTS)).astype(jnp.int32)
    test_matrix = centred(key_of[5], (R, POINTS), 1.0, 6.0, ((1, 256),))
    return {"queries": queries, "probe_group": probe_group, "probe_local": probe_local, "points": points, "point_cluster": point_cluster, "test_matrix": test_matrix}


def masked_scores(point_rows, point_ids, query_rows, query_ids):
    feature_width = point_rows.shape[1]
    block_rows = min(512, point_rows.shape[0])
    factor = feature_width ** (-0.5)

    def score_piece(pieces):
        piece_x, piece_ids = pieces
        product = lax.dot_general(piece_x, query_rows, (((1,), (1,)), ((), ())), preferred_element_type=jnp.float32) * factor
        return jnp.where(piece_ids[:, None] == query_ids[None, :], product, 0.0).astype(jnp.bfloat16)
    stacked = lax.map(score_piece, (point_rows.reshape(-1, block_rows, feature_width), point_ids.reshape(-1, block_rows)))
    return stacked.reshape(point_rows.shape[0], query_rows.shape[0])

def reference(queries, probe_group, probe_local, points, point_cluster, test_matrix):
    senders = QUERIES // QDEV
    per_sender = QDEV * PROBES
    target = probe_group.reshape(senders, per_sender)
    member = probe_local.reshape(-1)
    onehot_dest = (target[:, :, None] == jnp.arange(GROUPS, dtype=jnp.int32)[None, None, :]).astype(jnp.int32)
    ranking = lax.optimization_barrier(jnp.sum((jnp.cumsum(onehot_dest, axis=1).astype(jnp.int32) - onehot_dest) * onehot_dest, axis=2)).astype(jnp.int32)
    position = jnp.arange(senders, dtype=jnp.int32)[:, None] * CAP + ranking
    flat_index = jnp.arange(senders * per_sender, dtype=jnp.int32).reshape(senders, per_sender)
    slot_table = jnp.full((GROUPS, senders * CAP), -1, jnp.int32).at[target, position].set(flat_index)
    labels = jnp.arange(GCL, dtype=jnp.int32)

    def one_group(group_index):
        slot_index = slot_table[group_index]
        live_slot = slot_index >= 0
        safe_index = jnp.maximum(slot_index, 0)
        query_rows = jnp.where(live_slot[:, None], queries[safe_index // PROBES], jnp.zeros((), jnp.bfloat16))
        query_ids = jnp.where(live_slot, member[safe_index], -1)
        first_point = (group_index * GPOINTS).astype(jnp.int32)
        point_rows = lax.dynamic_slice_in_dim(points, first_point, GPOINTS, 0)
        point_ids = point_cluster[group_index]
        omega_rows = lax.dynamic_slice_in_dim(test_matrix, first_point, GPOINTS, 1)
        scores = masked_scores(point_rows, point_ids, query_rows, query_ids)
        lifted = jnp.dot(omega_rows, scores, preferred_element_type=jnp.float32).astype(jnp.bfloat16)
        product = lax.dot_general(lifted, scores, (((1,), (1,)), ((), ())), preferred_element_type=jnp.float32)
        query_hot = (query_ids[None, :] == labels[:, None]).astype(jnp.float32)
        point_hot = (point_ids[None, :] == labels[:, None]).astype(jnp.float32)
        queried = lax.optimization_barrier(jnp.sum(query_hot, axis=1))
        resident = lax.optimization_barrier(jnp.sum(point_hot, axis=1))
        factor = 1.0 / jnp.sqrt((queried + 1.0) * (queried + resident))
        sketch = product * lax.optimization_barrier(jnp.sum(factor[:, None] * point_hot, axis=0))[None, :]
        rounded = sketch.astype(jnp.bfloat16)
        weighted = (point_hot.astype(jnp.bfloat16)[:, None, :] * rounded[None, :, :]).reshape(GCL * R, GPOINTS)
        summed = jnp.dot(weighted, point_rows, preferred_element_type=jnp.float32).reshape(GCL, R, -1)
        regress = summed * (1.0 / jnp.sqrt(resident))[:, None, None]
        return (sketch, regress)
    sketches, regressors = lax.map(one_group, jnp.arange(GROUPS, dtype=jnp.int32))
    sketch_all = jnp.transpose(sketches, (1, 0, 2)).reshape(R, -1)
    return (sketch_all, regressors.reshape(-1, R, regressors.shape[3]))
```

```python
import jax
import jax.numpy as jnp
from jax import lax
from jax.sharding import PartitionSpec as P

F32 = jnp.float32
BF16 = jnp.bfloat16


def split(v):
    hi = v.astype(BF16)
    lo = (v - hi.astype(F32)).astype(BF16)
    return hi, lo


def dot2(v, w, dims):
    hi, lo = split(v)
    return lax.dot_general(hi, w, (dims, ((), ())), preferred_element_type=F32) + lax.dot_general(
        lo, w, (dims, ((), ())), preferred_element_type=F32
    )


def shards(queries, probe_group, probe_local, points, point_cluster, test_matrix):
    groups = lax.axis_size("shard")
    helpers = lax.axis_size("help")
    helper = lax.axis_index("help")
    rows, width = queries.shape
    probes = probe_group.shape[1]
    capacity = 2 * rows * probes // groups
    slots = groups * capacity
    rank = test_matrix.shape[0]
    own_points = points.shape[0]
    clusters = helpers
    scale = width ** (-0.5)

    target = probe_group.reshape(-1)
    hot = (target[:, None] == jnp.arange(groups, dtype=jnp.int32)[None, :]).astype(BF16)
    pairs = rows * probes
    before = (
        jnp.arange(pairs, dtype=jnp.int32)[:, None] > jnp.arange(pairs, dtype=jnp.int32)[None, :]
    ).astype(BF16)
    counts = jnp.dot(before, hot, preferred_element_type=F32)
    place = target * capacity + jnp.sum(counts * hot.astype(F32), axis=1).astype(jnp.int32)
    place = place.reshape(rows, probes)
    slot = jnp.arange(slots, dtype=jnp.int32)
    hit = [(slot[:, None] == place[:, k][None, :]) for k in range(probes)]
    packed = jnp.dot(
        (hit[0] | hit[1]).astype(BF16), queries, preferred_element_type=F32
    ).astype(BF16)
    ids = -1 + sum(
        jnp.sum(jnp.where(hit[k], probe_local[:, k][None, :] + 1, 0), axis=1) for k in range(probes)
    )
    pool = lax.all_to_all(
        packed.reshape(groups, capacity, width), "shard", split_axis=0, concat_axis=0, tiled=True
    ).reshape(slots, width)
    pool_ids = lax.all_to_all(
        ids.astype(jnp.int32).reshape(groups, 1, capacity), "shard", split_axis=0, concat_axis=0, tiled=True
    ).reshape(slots)

    group_ids = point_cluster[0]
    own_ids = lax.dynamic_slice_in_dim(group_ids, helper * own_points, own_points, 0)
    labels = jnp.arange(clusters, dtype=jnp.int32)
    resident = jnp.sum((group_ids[None, :] == labels[:, None]).astype(F32), axis=1)
    own_hot = own_ids[None, :] == labels[:, None]

    spread = jnp.where(own_hot[:, None, :], test_matrix[None], 0).reshape(clusters * rank, own_points)
    lead = lax.psum(jnp.dot(spread, points, preferred_element_type=F32), "help")
    lifted = dot2(lead * scale, pool, ((1,), (1,)))
    pool_hot = pool_ids[None, :] == labels[:, None]
    lifted = jnp.where(pool_hot[:, None, :], lifted.reshape(clusters, rank, slots), 0.0).reshape(
        clusters * rank, slots
    )
    back = dot2(lifted * scale, pool, ((1,), (0,)))
    named = jnp.sum(pool_hot.astype(F32), axis=1)
    back, queried = lax.psum((back, named), "help")
    product = dot2(back, points, ((1,), (1,))).reshape(clusters, rank, own_points)
    factor = 1.0 / jnp.sqrt((queried + 1.0) * (queried + resident))
    sketch = jnp.sum(jnp.where(own_hot[:, None, :], product * factor[:, None, None], 0.0), axis=0)
    rounded = sketch.astype(BF16)
    weighted = jnp.where(own_hot[:, None, :], rounded[None], 0).reshape(clusters * rank, own_points)
    summed = jnp.dot(weighted, points, preferred_element_type=F32)
    own = lax.psum_scatter(
        summed.reshape(clusters, rank, width), "help", scatter_dimension=0, tiled=True
    )
    own_scale = lax.dynamic_slice_in_dim(1.0 / jnp.sqrt(resident), helper, 1, 0)
    return (sketch, own * own_scale[:, None, None])


def solution(mesh):
    in_specs = (
        P(("shard", "help"), None),
        P(("shard", "help"), None),
        P(("shard", "help"), None),
        P(("shard", "help"), None),
        P("shard", None),
        P(None, ("shard", "help")),
    )
    out_specs = (P(None, ("shard", "help")), P(("shard", "help"), None, None))
    return jax.shard_map(shards, mesh=mesh, in_specs=in_specs, out_specs=out_specs, check_vma=False)
```

```python
import functools

import jax
import jax.numpy as jnp
from jax import lax
from jax.experimental import pallas as pl
from jax.experimental.pallas import tpu as pltpu
from jax.sharding import PartitionSpec as P

F32 = jnp.float32
BF16 = jnp.bfloat16
I32 = jnp.int32
MESH = pl.DeviceIdType.MESH
PLANE = 8
BACK = F32
FULL = F32
LAST = F32


def dot(a, b, ca, cb):
    return lax.dot_general(a, b, (((ca,), (cb,)), ((), ())), preferred_element_type=F32)


def stack_halves(v):
    hi = v.astype(BF16)
    lo = (v - hi.astype(F32)).astype(BF16)
    return jnp.concatenate([hi, lo], axis=0)


def dot_halves(v, w, cw):
    both = dot(stack_halves(v), w, 1, cw)
    n = v.shape[0]
    return both[:n] + both[n:]


def kernel(
    planes, helpers, capacity,
    group_hbm, local_hbm, query_hbm, point_hbm, cluster_hbm, test_hbm,
    sketch_hbm, regress_hbm,
    group, local, query, point, cluster, test,
    send, recv, tag_send, tag_recv,
    lead_part, lead_in, lead, count_part, count_in,
    back_part, back_in, back, last_part, last_in, sketch, regress,
    load_sem, row_send, row_recv, own_sem, tag_ssem, tag_rsem,
    lead_sem, lead2_sem, count_sem, back_sem, back2_sem, last_sem, out_sem,
):
    s = lax.axis_index("shard")
    h = lax.axis_index("help")
    z = s // PLANE
    spot = lax.rem(s, PLANE)
    groups = planes * PLANE
    rows, width = query.shape
    own_points = point.shape[0]
    rank = test.shape[0]
    slots = groups * capacity
    chunk = PLANE * capacity

    barrier = pltpu.get_barrier_semaphore()

    def greet(j, carry):
        pl.semaphore_signal(
            barrier, inc=1, device_id={"shard": lax.rem(s + j, groups)}, device_id_type=MESH
        )
        return carry

    lax.fori_loop(1, groups, greet, 0)
    for j in range(1, helpers):
        pl.semaphore_signal(
            barrier, inc=1, device_id={"help": lax.rem(h + j, helpers)}, device_id_type=MESH
        )

    loads = []
    for i, (a, b) in enumerate(
        ((group_hbm, group), (local_hbm, local), (query_hbm, query),
         (cluster_hbm, cluster), (test_hbm, test), (point_hbm, point))
    ):
        c = pltpu.make_async_copy(a, b, load_sem.at[i])
        c.start()
        loads.append(c)

    loads[0].wait()
    loads[1].wait()
    glabel = lax.broadcasted_iota(I32, (groups, rows), 0)
    hot = [glabel == group[k:k + 1, :] for k in range(2)]
    hotf = [m.astype(F32) for m in hot]
    earlier = (
        lax.broadcasted_iota(I32, (rows, rows), 0) < lax.broadcasted_iota(I32, (rows, rows), 1)
    ).astype(F32).astype(BF16)
    first_total = jnp.sum(hotf[0], axis=1, keepdims=True)
    before = [dot(hotf[k].astype(BF16), earlier, 1, 0) for k in range(2)]
    before[1] = before[1] + first_total
    order = [jnp.sum(hotf[k] * before[k], axis=0, keepdims=True).astype(I32) for k in range(2)]
    place = [group[k:k + 1, :] * capacity + order[k] for k in range(2)]
    lane = lax.broadcasted_iota(I32, (128, rows), 0)
    tags = sum(
        dot(
            (hotf[k] * (local[k:k + 1, :] + 1).astype(F32)).astype(BF16),
            (lane == order[k]).astype(F32).astype(BF16), 1, 1,
        )
        for k in range(2)
    )
    tag_send[...] = tags.reshape(groups, 1, 128)
    tag_recv[pl.ds(s, 1)] = tag_send[pl.ds(s, 1)]

    loads[2].wait()
    pl.semaphore_wait(barrier, groups - 1 + helpers - 1)

    def tag_copy(j, carry):
        t = lax.rem(s + j, groups)
        pltpu.make_async_remote_copy(
            src_ref=tag_send.at[t], dst_ref=tag_recv.at[s], send_sem=tag_ssem, recv_sem=tag_rsem,
            device_id={"shard": t}, device_id_type=MESH,
        ).start()
        return carry

    lax.fori_loop(1, groups, tag_copy, 0)

    far_first = sorted(range(planes), key=lambda d: -min(d, planes - d))
    slot = lax.broadcasted_iota(I32, (chunk, rows), 0)
    queries = query[...]
    for dz in far_first:
        zt = lax.rem(z + dz, planes)
        base = slot + zt * chunk
        pick = ((base == place[0]) | (base == place[1])).astype(F32).astype(BF16)
        packed = dot(pick, queries, 1, 0).astype(BF16)
        send[pl.ds(zt * PLANE, PLANE)] = packed.reshape(PLANE, capacity, width)

        def row_copy(e, carry, zt=zt, dz=dz):
            t = zt * PLANE + lax.rem(spot + e, PLANE)
            pltpu.make_async_remote_copy(
                src_ref=send.at[t], dst_ref=recv.at[s], send_sem=row_send, recv_sem=row_recv.at[dz],
                device_id={"shard": t}, device_id_type=MESH,
            ).start()
            return carry

        lax.fori_loop(1 if dz == 0 else 0, PLANE, row_copy, 0)
    own_copy = pltpu.make_async_copy(send.at[s], recv.at[s], own_sem)
    own_copy.start()

    def exchange(part, landing, sem):
        copies = []
        for j in range(1, helpers):
            t = lax.rem(h + j, helpers)
            copies.append(pltpu.make_async_remote_copy(
                src_ref=part.at[t], dst_ref=landing.at[j - 1],
                send_sem=sem.at[0, j - 1], recv_sem=sem.at[1, j - 1],
                device_id={"help": t}, device_id_type=MESH,
            ))
        for c in copies:
            c.start()
        return copies

    def publish(source, landing, sem):
        copies = []
        for j in range(1, helpers):
            t = lax.rem(h + j, helpers)
            copies.append(pltpu.make_async_remote_copy(
                src_ref=source, dst_ref=landing,
                send_sem=sem.at[0, j - 1], recv_sem=sem.at[1, j - 1],
                device_id={"help": t}, device_id_type=MESH,
            ))
        for c in copies:
            c.start()
        return copies

    def finish(copies):
        for c in copies:
            c.wait()

    for i in (3, 4, 5):
        loads[i].wait()
    mine = cluster[:, pl.ds(pl.multiple_of(h * own_points, own_points), own_points)]
    inside = [mine == c for c in range(helpers)]
    omega = test[...].astype(F32)
    spread = jnp.concatenate([jnp.where(m, omega, 0.0) for m in inside], axis=0).astype(BF16)
    lead_part[...] = dot(spread, point[...], 1, 0).reshape(helpers, rank, width)
    lead_copies = exchange(lead_part, lead_in, lead_sem)

    pltpu.make_async_remote_copy(
        src_ref=tag_send.at[pl.ds(0, groups - 1)], dst_ref=tag_recv.at[pl.ds(0, groups - 1)],
        send_sem=tag_ssem, recv_sem=tag_rsem,
        device_id={"shard": lax.rem(s + 1, groups)}, device_id_type=MESH,
    ).wait()
    tags = [tag_row(tag_recv, p, chunk, capacity) for p in range(planes)]
    named = [
        sum(jnp.sum((t == c + 1.0).astype(F32), axis=1, keepdims=True) for t in tags)
        for c in range(helpers)
    ]
    for c in range(helpers):
        count_part[c:c + 1, :] = jnp.broadcast_to(named[c], (1, 128))
    count_copies = []
    for j in range(1, helpers):
        c = pltpu.make_async_remote_copy(
            src_ref=count_part, dst_ref=count_in.at[j - 1],
            send_sem=count_sem.at[0, j - 1], recv_sem=count_sem.at[1, j - 1],
            device_id={"help": lax.rem(h + j, helpers)}, device_id_type=MESH,
        )
        c.start()
        count_copies.append(c)

    finish(lead_copies)
    total = lead_part[h]
    for j in range(helpers - 1):
        total = total + lead_in[j]
    lead[h] = total
    lead_copies = publish(lead.at[h], lead.at[h], lead2_sem)

    finish(count_copies)
    queried_all = count_part[...]
    for j in range(helpers - 1):
        queried_all = queried_all + count_in[j]
    everyone = cluster[...]
    factor = jnp.zeros((1, own_points), F32)
    for c in range(helpers):
        resident = jnp.sum((everyone == c).astype(F32), axis=1, keepdims=True)
        queried = queried_all[c:c + 1, 0:1]
        one = (1.0 / width) / jnp.sqrt((queried + 1.0) * (queried + resident))
        factor = jnp.where(inside[c], one, factor)
    own_resident = jnp.sum((everyone == h).astype(F32), axis=1, keepdims=True)
    own_scale = 1.0 / jnp.sqrt(own_resident)

    finish(lead_copies)
    halves = stack_halves(lead[...].reshape(helpers * rank, width))
    n = helpers * rank

    acc = jnp.zeros((2 * n, width), F32)
    for dz in sorted(range(planes), key=lambda d: min(d, planes - d)):
        zs = lax.rem(z + planes - dz, planes)
        k = PLANE - 1 if dz == 0 else PLANE
        pltpu.make_async_remote_copy(
            src_ref=send.at[pl.ds(0, k)], dst_ref=recv.at[pl.ds(0, k)],
            send_sem=row_send, recv_sem=row_recv.at[dz],
            device_id={"shard": lax.rem(s + 1, groups)}, device_id_type=MESH,
        ).wait_recv()
        if dz == 0:
            own_copy.wait()
        rowsy = recv[pl.ds(zs * PLANE, PLANE)].reshape(chunk, width)
        both = dot(halves, rowsy, 1, 1)
        lifted = both[:n] + both[n:]
        piece = tag_row(tag_recv, zs, chunk, capacity)
        lifted = jnp.concatenate(
            [jnp.where(piece == c + 1.0, lifted[c * rank:(c + 1) * rank], 0.0) for c in range(helpers)],
            axis=0,
        )
        acc = acc + dot(stack_halves(lifted), rowsy, 1, 0)
    product = (acc[:n] + acc[n:]).reshape(helpers, rank, width)
    back_part[...] = product.astype(BACK)
    back_copies = exchange(back_part, back_in, back_sem)
    finish(back_copies)
    total = back_part[h].astype(F32)
    for j in range(helpers - 1):
        total = total + back_in[j].astype(F32)
    back[h] = total.astype(FULL)
    finish(publish(back.at[h], back.at[h], back2_sem))

    full = back[...].reshape(n, width)
    points = point[...]
    if FULL == F32:
        wide = dot_halves(full, points, 1)
    else:
        wide = dot(full, points, 1, 1)
    chosen = wide[:rank]
    for c in range(1, helpers):
        chosen = jnp.where(inside[c], wide[c * rank:(c + 1) * rank], chosen)
    result = chosen * factor
    sketch[...] = result
    sketch_copy = pltpu.make_async_copy(sketch, sketch_hbm, out_sem.at[0])
    sketch_copy.start()
    rounded = result.astype(BF16).astype(F32)
    weighted = jnp.concatenate([jnp.where(m, rounded, 0.0) for m in inside], axis=0).astype(BF16)
    last_part[...] = dot(weighted, points, 1, 0).reshape(helpers, rank, width).astype(LAST)
    finish(exchange(last_part, last_in, last_sem))
    total = last_part[h].astype(F32)
    for j in range(helpers - 1):
        total = total + last_in[j].astype(F32)
    regress[...] = (total * own_scale).reshape(1, rank, width)
    regress_copy = pltpu.make_async_copy(regress, regress_hbm, out_sem.at[1])
    regress_copy.start()

    pltpu.make_async_remote_copy(
        src_ref=send.at[pl.ds(0, groups - 1)], dst_ref=recv.at[pl.ds(0, groups - 1)],
        send_sem=row_send, recv_sem=row_recv.at[0],
        device_id={"shard": lax.rem(s + 1, groups)}, device_id_type=MESH,
    ).wait_send()
    sketch_copy.wait()
    regress_copy.wait()


def tag_row(tag_recv, plane, chunk, capacity):
    part = tag_recv[pl.ds(plane * PLANE, PLANE)].reshape(PLANE, 128).astype(BF16)
    source = (
        lax.broadcasted_iota(I32, (PLANE, chunk), 0)
        == lax.broadcasted_iota(I32, (PLANE, chunk), 1) // capacity
    ).astype(F32).astype(BF16)
    wide = dot(part, source, 0, 0)[:capacity]
    return jnp.sum(
        jnp.where(
            lax.broadcasted_iota(I32, (capacity, chunk), 0)
            == lax.rem(lax.broadcasted_iota(I32, (capacity, chunk), 1), capacity),
            wide, 0.0,
        ),
        axis=0, keepdims=True,
    )


def shards(queries, probe_group, probe_local, points, point_cluster, test_matrix):
    groups = lax.axis_size("shard")
    helpers = lax.axis_size("help")
    rows, width = queries.shape
    probes = probe_group.shape[1]
    capacity = 2 * rows * probes // groups
    own_points = points.shape[0]
    rank = test_matrix.shape[0]
    planes = groups // PLANE
    peers = helpers - 1
    slab = (helpers, rank, width)
    away = (peers, rank, width)
    DMA = pltpu.SemaphoreType.DMA
    return pl.pallas_call(
        functools.partial(kernel, planes, helpers, capacity),
        out_shape=(
            jax.ShapeDtypeStruct((rank, own_points), F32),
            jax.ShapeDtypeStruct((1, rank, width), F32),
        ),
        in_specs=[pl.BlockSpec(memory_space=pl.ANY)] * 6,
        out_specs=(pl.BlockSpec(memory_space=pl.ANY), pl.BlockSpec(memory_space=pl.ANY)),
        scratch_shapes=[
            pltpu.VMEM((probes, rows), I32),
            pltpu.VMEM((probes, rows), I32),
            pltpu.VMEM((rows, width), BF16),
            pltpu.VMEM((own_points, width), BF16),
            pltpu.VMEM(point_cluster.shape, I32),
            pltpu.VMEM((rank, own_points), BF16),
            pltpu.VMEM((groups, capacity, width), BF16),
            pltpu.VMEM((groups, capacity, width), BF16),
            pltpu.VMEM((groups, 1, 128), F32),
            pltpu.VMEM((groups, 1, 128), F32),
            pltpu.VMEM(slab, F32),
            pltpu.VMEM(away, F32),
            pltpu.VMEM(slab, F32),
            pltpu.VMEM((helpers, 128), F32),
            pltpu.VMEM((peers, helpers, 128), F32),
            pltpu.VMEM(slab, BACK),
            pltpu.VMEM(away, BACK),
            pltpu.VMEM(slab, FULL),
            pltpu.VMEM(slab, LAST),
            pltpu.VMEM(away, LAST),
            pltpu.VMEM((rank, own_points), F32),
            pltpu.VMEM((1, rank, width), F32),
            DMA((6,)),
            DMA,
            DMA((planes,)),
            DMA,
            DMA,
            DMA,
            DMA((2, peers)),
            DMA((2, peers)),
            DMA((2, peers)),
            DMA((2, peers)),
            DMA((2, peers)),
            DMA((2, peers)),
            DMA((2,)),
        ],
        compiler_params=pltpu.CompilerParams(collective_id=0, has_side_effects=True),
    )(probe_group.T, probe_local.T, queries, points, point_cluster, test_matrix)


def solution(mesh):
    in_specs = (
        P(("shard", "help"), None),
        P(("shard", "help"), None),
        P(("shard", "help"), None),
        P(("shard", "help"), None),
        P("shard", None),
        P(None, ("shard", "help")),
    )
    out_specs = (P(None, ("shard", "help")), P(("shard", "help"), None, None))
    return jax.shard_map(shards, mesh=mesh, in_specs=in_specs, out_specs=out_specs, check_vma=False)
```

```python
import functools

import jax
import jax.numpy as jnp
from jax import lax
from jax.experimental import pallas as pl
from jax.experimental.pallas import tpu as pltpu
from jax.sharding import PartitionSpec as P

F32 = jnp.float32
BF16 = jnp.bfloat16
I32 = jnp.int32
MESH = pl.DeviceIdType.MESH
PLANE = 8
BACK = BF16
FULL = BF16
LAST = BF16


def dot(a, b, ca, cb):
    return lax.dot_general(a, b, (((ca,), (cb,)), ((), ())), preferred_element_type=F32)


def stack_halves(v):
    hi = v.astype(BF16)
    lo = (v - hi.astype(F32)).astype(BF16)
    return jnp.concatenate([hi, lo], axis=0)


def dot_halves(v, w, cw):
    both = dot(stack_halves(v), w, 1, cw)
    n = v.shape[0]
    return both[:n] + both[n:]


def kernel(
    planes, helpers, capacity,
    group_hbm, local_hbm, query_hbm, point_hbm, cluster_hbm, test_hbm,
    sketch_hbm, regress_hbm,
    group, local, query, point, cluster, test,
    send, recv, tag_send, tag_recv,
    lead_part, lead_in, lead, count_part, count_in,
    back_part, back_in, back, last_part, last_in, sketch, regress,
    load_sem, row_send, row_recv, own_sem, tag_ssem, tag_rsem,
    lead_sem, lead2_sem, count_sem, back_sem, back2_sem, last_sem, out_sem, round_sem,
):
    s = lax.axis_index("shard")
    h = lax.axis_index("help")
    z = s // PLANE
    spot = lax.rem(s, PLANE)
    groups = planes * PLANE
    rows, width = query.shape
    own_points = point.shape[0]
    rank = test.shape[0]
    slots = groups * capacity
    chunk = PLANE * capacity

    barrier = pltpu.get_barrier_semaphore()

    column = sorted({1, planes - 1})

    def greet(j, carry):
        pl.semaphore_signal(
            barrier, inc=1, device_id={"shard": z * PLANE + lax.rem(spot + j, PLANE)},
            device_id_type=MESH,
        )
        return carry

    def call_column(ref):
        for i, d in enumerate(column):
            pl.semaphore_signal(
                ref(i), inc=1, device_id={"shard": lax.rem(s + d * PLANE, groups)},
                device_id_type=MESH,
            )

    call_column(lambda i: barrier)
    lax.fori_loop(1, PLANE, greet, 0)
    for j in range(1, helpers):
        pl.semaphore_signal(
            barrier, inc=1, device_id={"help": lax.rem(h + j, helpers)}, device_id_type=MESH
        )

    loads = []
    for i, (a, b) in enumerate(
        ((group_hbm, group), (local_hbm, local), (query_hbm, query),
         (cluster_hbm, cluster), (test_hbm, test), (point_hbm, point))
    ):
        c = pltpu.make_async_copy(a, b, load_sem.at[i])
        c.start()
        loads.append(c)

    loads[0].wait()
    loads[1].wait()
    glabel = lax.broadcasted_iota(I32, (groups, rows), 0)
    hot = [glabel == group[k:k + 1, :] for k in range(2)]
    hotf = [m.astype(F32) for m in hot]
    earlier = (
        lax.broadcasted_iota(I32, (rows, rows), 0) < lax.broadcasted_iota(I32, (rows, rows), 1)
    ).astype(F32).astype(BF16)
    first_total = jnp.sum(hotf[0], axis=1, keepdims=True)
    before = [dot(hotf[k].astype(BF16), earlier, 1, 0) for k in range(2)]
    before[1] = before[1] + first_total
    order = [jnp.sum(hotf[k] * before[k], axis=0, keepdims=True).astype(I32) for k in range(2)]
    place = [group[k:k + 1, :] * capacity + order[k] for k in range(2)]
    lane = lax.broadcasted_iota(I32, (128, rows), 0)
    tags = sum(
        dot(
            (hotf[k] * (local[k:k + 1, :] + 1).astype(F32)).astype(BF16),
            (lane == order[k]).astype(F32).astype(BF16), 1, 1,
        )
        for k in range(2)
    )
    tag_send[...] = tags.reshape(groups, 1, 128)
    tag_recv[pl.ds(s, 1)] = tag_send[pl.ds(s, 1)]

    loads[2].wait()
    slot = lax.broadcasted_iota(I32, (chunk, rows), 0)
    queries = query[...]

    def pack(dz):
        zt = lax.rem(z + dz, planes)
        base = slot + zt * chunk
        pick = ((base == place[0]) | (base == place[1])).astype(F32).astype(BF16)
        packed = dot(pick, queries, 1, 0).astype(BF16)
        send[pl.ds(zt * PLANE, PLANE)] = packed.reshape(PLANE, capacity, width)

    def ship(dz):
        zt = lax.rem(z + dz, planes)

        def tag_copy(e, carry):
            t = zt * PLANE + lax.rem(spot + e, PLANE)
            pltpu.make_async_remote_copy(
                src_ref=tag_send.at[t], dst_ref=tag_recv.at[s],
                send_sem=tag_ssem, recv_sem=tag_rsem.at[dz],
                device_id={"shard": t}, device_id_type=MESH,
            ).start()
            return carry

        def row_copy(e, carry):
            t = zt * PLANE + lax.rem(spot + e, PLANE)
            pltpu.make_async_remote_copy(
                src_ref=send.at[t], dst_ref=recv.at[s],
                send_sem=row_send, recv_sem=row_recv.at[dz],
                device_id={"shard": t}, device_id_type=MESH,
            ).start()
            return carry

        low = 1 if dz == 0 else 0
        lax.fori_loop(low, PLANE, tag_copy, 0)
        lax.fori_loop(low, PLANE, row_copy, 0)

    pack(0)
    for d in column:
        pack(d)
    pl.semaphore_wait(barrier, len(column) + PLANE - 1 + helpers - 1)
    for far in range(planes // 2 + 1):
        if far > 0:
            for i in range(len(column)):
                pl.semaphore_wait(round_sem.at[far - 1, i], 1)
        if far < planes // 2:
            call_column(lambda i, far=far: round_sem.at[far, i])
        for dz in sorted({far % planes, (planes - far) % planes}):
            if far > 1:
                pack(dz)
            ship(dz)
    own_copy = pltpu.make_async_copy(send.at[s], recv.at[s], own_sem)
    own_copy.start()

    def exchange(part, landing, sem):
        copies = []
        for j in range(1, helpers):
            t = lax.rem(h + j, helpers)
            copies.append(pltpu.make_async_remote_copy(
                src_ref=part.at[t], dst_ref=landing.at[j - 1],
                send_sem=sem.at[0, j - 1], recv_sem=sem.at[1, j - 1],
                device_id={"help": t}, device_id_type=MESH,
            ))
        for c in copies:
            c.start()
        return copies

    def publish(source, landing, sem):
        copies = []
        for j in range(1, helpers):
            t = lax.rem(h + j, helpers)
            copies.append(pltpu.make_async_remote_copy(
                src_ref=source, dst_ref=landing,
                send_sem=sem.at[0, j - 1], recv_sem=sem.at[1, j - 1],
                device_id={"help": t}, device_id_type=MESH,
            ))
        for c in copies:
            c.start()
        return copies

    def finish(copies):
        for c in copies:
            c.wait()

    for i in (3, 4, 5):
        loads[i].wait()
    mine = cluster[:, pl.ds(pl.multiple_of(h * own_points, own_points), own_points)]
    inside = [mine == c for c in range(helpers)]
    omega = test[...].astype(F32)
    spread = jnp.concatenate([jnp.where(m, omega, 0.0) for m in inside], axis=0).astype(BF16)
    lead_part[...] = dot(spread, point[...], 1, 0).reshape(helpers, rank, width)
    lead_copies = exchange(lead_part, lead_in, lead_sem)

    finish(lead_copies)
    total = lead_part[h]
    for j in range(helpers - 1):
        total = total + lead_in[j]
    lead[h] = total
    lead_copies = publish(lead.at[h], lead.at[h], lead2_sem)

    everyone = cluster[...]
    residents = [
        jnp.sum((everyone == c).astype(F32), axis=1, keepdims=True) for c in range(helpers)
    ]
    own_resident = jnp.sum((everyone == h).astype(F32), axis=1, keepdims=True)
    own_scale = 1.0 / jnp.sqrt(own_resident)

    finish(lead_copies)
    halves = stack_halves(lead[...].reshape(helpers * rank, width))
    n = helpers * rank

    acc = jnp.zeros((2 * n, width), F32)
    named = [jnp.zeros((1, 1), F32) for c in range(helpers)]
    for dz in sorted(range(planes), key=lambda d: min(d, planes - d)):
        zs = lax.rem(z + planes - dz, planes)
        k = PLANE - 1 if dz == 0 else PLANE
        pltpu.make_async_remote_copy(
            src_ref=send.at[pl.ds(0, k)], dst_ref=recv.at[pl.ds(0, k)],
            send_sem=row_send, recv_sem=row_recv.at[dz],
            device_id={"shard": lax.rem(s + 1, groups)}, device_id_type=MESH,
        ).wait_recv()
        pltpu.make_async_remote_copy(
            src_ref=tag_send.at[pl.ds(0, k)], dst_ref=tag_recv.at[pl.ds(0, k)],
            send_sem=tag_ssem, recv_sem=tag_rsem.at[dz],
            device_id={"shard": lax.rem(s + 1, groups)}, device_id_type=MESH,
        ).wait_recv()
        if dz == 0:
            own_copy.wait()
        rowsy = recv[pl.ds(zs * PLANE, PLANE)].reshape(chunk, width)
        both = dot(halves, rowsy, 1, 1)
        lifted = both[:n] + both[n:]
        piece = tag_row(tag_recv, zs, chunk, capacity)
        named = [
            named[c] + jnp.sum((piece == c + 1.0).astype(F32), axis=1, keepdims=True)
            for c in range(helpers)
        ]
        lifted = jnp.concatenate(
            [jnp.where(piece == c + 1.0, lifted[c * rank:(c + 1) * rank], 0.0) for c in range(helpers)],
            axis=0,
        )
        acc = acc + dot(stack_halves(lifted), rowsy, 1, 0)
    product = (acc[:n] + acc[n:]).reshape(helpers, rank, width)
    back_part[...] = product.astype(BACK)
    back_copies = exchange(back_part, back_in, back_sem)
    for c in range(helpers):
        count_part[c:c + 1, :] = jnp.broadcast_to(named[c], (1, 128))
    count_copies = []
    for j in range(1, helpers):
        c = pltpu.make_async_remote_copy(
            src_ref=count_part, dst_ref=count_in.at[j - 1],
            send_sem=count_sem.at[0, j - 1], recv_sem=count_sem.at[1, j - 1],
            device_id={"help": lax.rem(h + j, helpers)}, device_id_type=MESH,
        )
        c.start()
        count_copies.append(c)
    finish(back_copies)
    total = back_part[h].astype(F32)
    for j in range(helpers - 1):
        total = total + back_in[j].astype(F32)
    back[h] = total.astype(FULL)
    back_copies = publish(back.at[h], back.at[h], back2_sem)
    finish(count_copies)
    queried_all = count_part[...]
    for j in range(helpers - 1):
        queried_all = queried_all + count_in[j]
    factor = jnp.zeros((1, own_points), F32)
    for c in range(helpers):
        queried = queried_all[c:c + 1, 0:1]
        one = (1.0 / width) / jnp.sqrt((queried + 1.0) * (queried + residents[c]))
        factor = jnp.where(inside[c], one, factor)
    finish(back_copies)

    full = back[...].reshape(n, width)
    points = point[...]
    if FULL == F32:
        wide = dot_halves(full, points, 1)
    else:
        wide = dot(full, points, 1, 1)
    chosen = wide[:rank]
    for c in range(1, helpers):
        chosen = jnp.where(inside[c], wide[c * rank:(c + 1) * rank], chosen)
    result = chosen * factor
    sketch[...] = result
    sketch_copy = pltpu.make_async_copy(sketch, sketch_hbm, out_sem.at[0])
    sketch_copy.start()
    rounded = result.astype(BF16).astype(F32)
    weighted = jnp.concatenate([jnp.where(m, rounded, 0.0) for m in inside], axis=0).astype(BF16)
    last_part[...] = dot(weighted, points, 1, 0).reshape(helpers, rank, width).astype(LAST)
    finish(exchange(last_part, last_in, last_sem))
    total = last_part[h].astype(F32)
    for j in range(helpers - 1):
        total = total + last_in[j].astype(F32)
    regress[...] = (total * own_scale).reshape(1, rank, width)
    regress_copy = pltpu.make_async_copy(regress, regress_hbm, out_sem.at[1])
    regress_copy.start()

    pltpu.make_async_remote_copy(
        src_ref=send.at[pl.ds(0, groups - 1)], dst_ref=recv.at[pl.ds(0, groups - 1)],
        send_sem=row_send, recv_sem=row_recv.at[0],
        device_id={"shard": lax.rem(s + 1, groups)}, device_id_type=MESH,
    ).wait_send()
    pltpu.make_async_remote_copy(
        src_ref=tag_send.at[pl.ds(0, groups - 1)], dst_ref=tag_recv.at[pl.ds(0, groups - 1)],
        send_sem=tag_ssem, recv_sem=tag_rsem.at[0],
        device_id={"shard": lax.rem(s + 1, groups)}, device_id_type=MESH,
    ).wait_send()
    sketch_copy.wait()
    regress_copy.wait()


def tag_row(tag_recv, plane, chunk, capacity):
    part = tag_recv[pl.ds(plane * PLANE, PLANE)].reshape(PLANE, 128).astype(BF16)
    source = (
        lax.broadcasted_iota(I32, (PLANE, chunk), 0)
        == lax.broadcasted_iota(I32, (PLANE, chunk), 1) // capacity
    ).astype(F32).astype(BF16)
    wide = dot(part, source, 0, 0)[:capacity]
    return jnp.sum(
        jnp.where(
            lax.broadcasted_iota(I32, (capacity, chunk), 0)
            == lax.rem(lax.broadcasted_iota(I32, (capacity, chunk), 1), capacity),
            wide, 0.0,
        ),
        axis=0, keepdims=True,
    )


def shards(queries, probe_group, probe_local, points, point_cluster, test_matrix):
    groups = lax.axis_size("shard")
    helpers = lax.axis_size("help")
    rows, width = queries.shape
    probes = probe_group.shape[1]
    capacity = 2 * rows * probes // groups
    own_points = points.shape[0]
    rank = test_matrix.shape[0]
    planes = groups // PLANE
    peers = helpers - 1
    slab = (helpers, rank, width)
    away = (peers, rank, width)
    DMA = pltpu.SemaphoreType.DMA
    return pl.pallas_call(
        functools.partial(kernel, planes, helpers, capacity),
        out_shape=(
            jax.ShapeDtypeStruct((rank, own_points), F32),
            jax.ShapeDtypeStruct((1, rank, width), F32),
        ),
        in_specs=[pl.BlockSpec(memory_space=pl.ANY)] * 6,
        out_specs=(pl.BlockSpec(memory_space=pl.ANY), pl.BlockSpec(memory_space=pl.ANY)),
        scratch_shapes=[
            pltpu.VMEM((probes, rows), I32),
            pltpu.VMEM((probes, rows), I32),
            pltpu.VMEM((rows, width), BF16),
            pltpu.VMEM((own_points, width), BF16),
            pltpu.VMEM(point_cluster.shape, I32),
            pltpu.VMEM((rank, own_points), BF16),
            pltpu.VMEM((groups, capacity, width), BF16),
            pltpu.VMEM((groups, capacity, width), BF16),
            pltpu.VMEM((groups, 1, 128), F32),
            pltpu.VMEM((groups, 1, 128), F32),
            pltpu.VMEM(slab, F32),
            pltpu.VMEM(away, F32),
            pltpu.VMEM(slab, F32),
            pltpu.VMEM((helpers, 128), F32),
            pltpu.VMEM((peers, helpers, 128), F32),
            pltpu.VMEM(slab, BACK),
            pltpu.VMEM(away, BACK),
            pltpu.VMEM(slab, FULL),
            pltpu.VMEM(slab, LAST),
            pltpu.VMEM(away, LAST),
            pltpu.VMEM((rank, own_points), F32),
            pltpu.VMEM((1, rank, width), F32),
            DMA((6,)),
            DMA,
            DMA((planes,)),
            DMA,
            DMA,
            DMA((planes,)),
            DMA((2, peers)),
            DMA((2, peers)),
            DMA((2, peers)),
            DMA((2, peers)),
            DMA((2, peers)),
            DMA((2, peers)),
            DMA((2,)),
            pltpu.SemaphoreType.REGULAR((planes // 2, 2)),
        ],
        compiler_params=pltpu.CompilerParams(collective_id=0, has_side_effects=True),
    )(probe_group.T, probe_local.T, queries, points, point_cluster, test_matrix)


def solution(mesh):
    in_specs = (
        P(("shard", "help"), None),
        P(("shard", "help"), None),
        P(("shard", "help"), None),
        P(("shard", "help"), None),
        P("shard", None),
        P(None, ("shard", "help")),
    )
    out_specs = (P(None, ("shard", "help")), P(("shard", "help"), None, None))
    return jax.shard_map(shards, mesh=mesh, in_specs=in_specs, out_specs=out_specs, check_vma=False)
```

```python
import functools

import jax
import jax.numpy as jnp
from jax import lax
from jax.experimental import pallas as pl
from jax.experimental.pallas import tpu as pltpu
from jax.sharding import PartitionSpec as P

F32 = jnp.float32
BF16 = jnp.bfloat16
I32 = jnp.int32
MESH = pl.DeviceIdType.MESH
PLANE = 8
BACK = BF16
FULL = BF16
LAST = BF16


def dot(a, b, ca, cb):
    return lax.dot_general(a, b, (((ca,), (cb,)), ((), ())), preferred_element_type=F32)


def stack_halves(v):
    hi = v.astype(BF16)
    lo = (v - hi.astype(F32)).astype(BF16)
    return jnp.concatenate([hi, lo], axis=0)


def dot_halves(v, w, cw):
    both = dot(stack_halves(v), w, 1, cw)
    n = v.shape[0]
    return both[:n] + both[n:]


def kernel(
    planes, helpers, capacity,
    group_hbm, local_hbm, query_hbm, point_hbm, cluster_hbm, test_hbm,
    sketch_hbm, regress_hbm,
    group, local, query, point, cluster, test,
    send, recv, tag_send, tag_recv,
    lead_part, lead_in, lead, count_part, count_in,
    back_part, back_in, back, last_part, last_in, sketch, regress,
    load_sem, row_send, row_recv, own_sem, tag_ssem, tag_rsem,
    lead_sem, lead2_sem, count_sem, back_sem, back2_sem, last_sem, out_sem, round_sem,
    far_rows, far_tags, far_lead, far_back, far_count,
    share_sem, stag_sem, flead_sem, fback_sem, fcount_sem,
):
    s = lax.axis_index("shard")
    h = lax.axis_index("help")
    z = s // PLANE
    spot = lax.rem(s, PLANE)
    groups = planes * PLANE
    rows, width = query.shape
    own_points = point.shape[0]
    rank = test.shape[0]
    slots = groups * capacity
    chunk = PLANE * capacity

    barrier = pltpu.get_barrier_semaphore()

    column = sorted({1, planes - 1})

    def greet(j, carry):
        pl.semaphore_signal(
            barrier, inc=1, device_id={"shard": z * PLANE + lax.rem(spot + j, PLANE)},
            device_id_type=MESH,
        )
        return carry

    def call_column(ref):
        for i, d in enumerate(column):
            pl.semaphore_signal(
                ref(i), inc=1, device_id={"shard": lax.rem(s + d * PLANE, groups)},
                device_id_type=MESH,
            )

    call_column(lambda i: barrier)
    lax.fori_loop(1, PLANE, greet, 0)
    for j in range(1, helpers):
        pl.semaphore_signal(
            barrier, inc=1, device_id={"help": lax.rem(h + j, helpers)}, device_id_type=MESH
        )

    loads = []
    for i, (a, b) in enumerate(
        ((group_hbm, group), (local_hbm, local), (query_hbm, query),
         (cluster_hbm, cluster), (test_hbm, test), (point_hbm, point))
    ):
        c = pltpu.make_async_copy(a, b, load_sem.at[i])
        c.start()
        loads.append(c)

    loads[0].wait()
    loads[1].wait()
    glabel = lax.broadcasted_iota(I32, (groups, rows), 0)
    hot = [glabel == group[k:k + 1, :] for k in range(2)]
    hotf = [m.astype(F32) for m in hot]
    earlier = (
        lax.broadcasted_iota(I32, (rows, rows), 0) < lax.broadcasted_iota(I32, (rows, rows), 1)
    ).astype(F32).astype(BF16)
    first_total = jnp.sum(hotf[0], axis=1, keepdims=True)
    before = [dot(hotf[k].astype(BF16), earlier, 1, 0) for k in range(2)]
    before[1] = before[1] + first_total
    order = [jnp.sum(hotf[k] * before[k], axis=0, keepdims=True).astype(I32) for k in range(2)]
    place = [group[k:k + 1, :] * capacity + order[k] for k in range(2)]
    lane = lax.broadcasted_iota(I32, (128, rows), 0)
    tags = sum(
        dot(
            (hotf[k] * (local[k:k + 1, :] + 1).astype(F32)).astype(BF16),
            (lane == order[k]).astype(F32).astype(BF16), 1, 1,
        )
        for k in range(2)
    )
    tag_send[...] = tags.reshape(groups, 1, 128)
    opposite = planes // 2
    zo = lax.rem(z + opposite, planes)
    across = zo * PLANE + spot
    tag_recv[pl.ds(s, 1)] = tag_send[pl.ds(s, 1)]
    tag_recv[pl.ds(across, 1)] = tag_send[pl.ds(across, 1)]

    loads[2].wait()
    slot = lax.broadcasted_iota(I32, (chunk, rows), 0)
    queries = query[...]

    def pack(dz):
        zt = lax.rem(z + dz, planes)
        base = slot + zt * chunk
        pick = ((base == place[0]) | (base == place[1])).astype(F32).astype(BF16)
        packed = dot(pick, queries, 1, 0).astype(BF16)
        send[pl.ds(zt * PLANE, PLANE)] = packed.reshape(PLANE, capacity, width)

    def ship(dz):
        zt = lax.rem(z + dz, planes)
        zd = z if dz == opposite else zt
        slot_there = across if dz == opposite else s

        def tag_copy(e, carry):
            t = lax.rem(spot + e, PLANE)
            pltpu.make_async_remote_copy(
                src_ref=tag_send.at[zt * PLANE + t], dst_ref=tag_recv.at[slot_there],
                send_sem=tag_ssem, recv_sem=tag_rsem.at[dz],
                device_id={"shard": zd * PLANE + t}, device_id_type=MESH,
            ).start()
            return carry

        def row_copy(e, carry):
            t = lax.rem(spot + e, PLANE)
            pltpu.make_async_remote_copy(
                src_ref=send.at[zt * PLANE + t], dst_ref=recv.at[slot_there],
                send_sem=row_send, recv_sem=row_recv.at[dz],
                device_id={"shard": zd * PLANE + t}, device_id_type=MESH,
            ).start()
            return carry

        low = 1 if dz in (0, opposite) else 0
        lax.fori_loop(low, PLANE, tag_copy, 0)
        lax.fori_loop(low, PLANE, row_copy, 0)

    pack(0)
    pack(opposite)
    near = [d for d in column if d != opposite]
    for d in near:
        pack(d)
    pl.semaphore_wait(barrier, len(column) + PLANE - 1 + helpers - 1)
    call_column(lambda i: round_sem.at[0, i])
    ship(0)
    ship(opposite)
    own_copy = pltpu.make_async_copy(send.at[s], recv.at[s], own_sem.at[0])
    own_copy.start()
    across_copy = pltpu.make_async_copy(send.at[across], recv.at[across], own_sem.at[1])
    across_copy.start()

    def advance(far):
        for i in range(len(column)):
            pl.semaphore_wait(round_sem.at[far - 1, i], 1)
        if far < opposite:
            call_column(lambda i: round_sem.at[far, i])

    def arrived(dz, k):
        pltpu.make_async_remote_copy(
            src_ref=send.at[pl.ds(0, k)], dst_ref=recv.at[pl.ds(0, k)],
            send_sem=row_send, recv_sem=row_recv.at[dz],
            device_id={"shard": lax.rem(s + 1, groups)}, device_id_type=MESH,
        ).wait_recv()
        pltpu.make_async_remote_copy(
            src_ref=tag_send.at[pl.ds(0, k)], dst_ref=tag_recv.at[pl.ds(0, k)],
            send_sem=tag_ssem, recv_sem=tag_rsem.at[dz],
            device_id={"shard": lax.rem(s + 1, groups)}, device_id_type=MESH,
        ).wait_recv()

    advance(1)
    for d in near:
        ship(d)

    def exchange(part, landing, sem):
        copies = []
        for j in range(1, helpers):
            t = lax.rem(h + j, helpers)
            copies.append(pltpu.make_async_remote_copy(
                src_ref=part.at[t], dst_ref=landing.at[j - 1],
                send_sem=sem.at[0, j - 1], recv_sem=sem.at[1, j - 1],
                device_id={"help": t}, device_id_type=MESH,
            ))
        for c in copies:
            c.start()
        return copies

    def publish(source, landing, sem):
        copies = []
        for j in range(1, helpers):
            t = lax.rem(h + j, helpers)
            copies.append(pltpu.make_async_remote_copy(
                src_ref=source, dst_ref=landing,
                send_sem=sem.at[0, j - 1], recv_sem=sem.at[1, j - 1],
                device_id={"help": t}, device_id_type=MESH,
            ))
        for c in copies:
            c.start()
        return copies

    def finish(copies):
        for c in copies:
            c.wait()

    for i in (3, 4, 5):
        loads[i].wait()
    mine = cluster[:, pl.ds(pl.multiple_of(h * own_points, own_points), own_points)]
    inside = [mine == c for c in range(helpers)]
    omega = test[...].astype(F32)
    spread = jnp.concatenate([jnp.where(m, omega, 0.0) for m in inside], axis=0).astype(BF16)
    lead_part[...] = dot(spread, point[...], 1, 0).reshape(helpers, rank, width)
    lead_copies = exchange(lead_part, lead_in, lead_sem)

    for far in range(2, opposite + 1):
        advance(far)
        if far < opposite:
            for dz in (far, planes - far):
                pack(dz)
                if far < opposite - 1 or far == 2:
                    ship(dz)

    def to_opposite(pair, sem):
        c = pltpu.make_async_remote_copy(
            src_ref=pair.at[0], dst_ref=pair.at[1], send_sem=sem.at[0], recv_sem=sem.at[1],
            device_id={"shard": across}, device_id_type=MESH,
        )
        c.start()
        return c

    arrived(opposite, PLANE - 1)
    across_copy.wait()
    shared = []
    for j in range(1, helpers):
        for a, b, sem in ((recv, far_rows, share_sem), (tag_recv, far_tags, stag_sem)):
            c = pltpu.make_async_remote_copy(
                src_ref=a.at[pl.ds(zo * PLANE, PLANE)], dst_ref=b.at[j - 1],
                send_sem=sem.at[0, j - 1], recv_sem=sem.at[1, j - 1],
                device_id={"help": lax.rem(h + j, helpers)}, device_id_type=MESH,
            )
            c.start()
            shared.append(c)
    far_piece = tag_row(tag_recv[pl.ds(zo * PLANE, PLANE)], chunk, capacity)
    for c in range(helpers):
        far_count[0, c:c + 1, :] = jnp.broadcast_to(
            jnp.sum((far_piece == c + 1.0).astype(F32), axis=1, keepdims=True), (1, 128)
        )
    count_move = to_opposite(far_count, fcount_sem)

    finish(lead_copies)
    total = lead_part[h]
    for j in range(helpers - 1):
        total = total + lead_in[j]
    far_lead[0] = total.astype(BF16)
    lead[h] = total
    lead_move = to_opposite(far_lead, flead_sem)
    lead_copies = publish(lead.at[h], lead.at[h], lead2_sem)
    if opposite - 1 > 2:
        for dz in (opposite - 1, opposite + 1):
            ship(dz)

    everyone = cluster[...]
    residents = [
        jnp.sum((everyone == c).astype(F32), axis=1, keepdims=True) for c in range(helpers)
    ]
    own_resident = jnp.sum((everyone == h).astype(F32), axis=1, keepdims=True)
    own_scale = 1.0 / jnp.sqrt(own_resident)

    finish(lead_copies)
    halves = stack_halves(lead[...].reshape(helpers * rank, width))
    n = helpers * rank

    acc = jnp.zeros((2 * n, width), F32)
    named = [jnp.zeros((1, 1), F32) for c in range(helpers)]

    def far_product():
        lead_move.wait()
        finish(shared)
        lead_there = far_lead[1]
        label = h.astype(F32) + 1.0
        got = jnp.zeros((2 * rank, width), F32)
        for j in range(helpers):
            if j == 0:
                far_r, piece = recv[pl.ds(zo * PLANE, PLANE)], far_piece
            else:
                far_r, piece = far_rows[j - 1], tag_row(far_tags[j - 1], chunk, capacity)
            far_r = far_r.reshape(chunk, width)
            lifted = jnp.where(piece == label, dot(lead_there, far_r, 1, 1), 0.0)
            got = got + dot(stack_halves(lifted), far_r, 1, 0)
        far_back[0] = (got[:rank] + got[rank:]).astype(BF16)
        return to_opposite(far_back, fback_sem)

    back_move = None
    for dz in sorted([d for d in range(planes) if d != opposite], key=lambda d: min(d, planes - d)):
        if back_move is None and min(dz, planes - dz) == max(opposite - 1, 1):
            back_move = far_product()
        zs = lax.rem(z + planes - dz, planes)
        arrived(dz, PLANE - 1 if dz == 0 else PLANE)
        if dz == 0:
            own_copy.wait()
        rowsy = recv[pl.ds(zs * PLANE, PLANE)].reshape(chunk, width)
        both = dot(halves, rowsy, 1, 1)
        lifted = both[:n] + both[n:]
        piece = tag_row(tag_recv[pl.ds(zs * PLANE, PLANE)], chunk, capacity)
        named = [
            named[c] + jnp.sum((piece == c + 1.0).astype(F32), axis=1, keepdims=True)
            for c in range(helpers)
        ]
        lifted = jnp.concatenate(
            [jnp.where(piece == c + 1.0, lifted[c * rank:(c + 1) * rank], 0.0) for c in range(helpers)],
            axis=0,
        )
        acc = acc + dot(stack_halves(lifted), rowsy, 1, 0)
    if back_move is None:
        back_move = far_product()
    count_move.wait()
    product = (acc[:n] + acc[n:]).reshape(helpers, rank, width)
    back_part[...] = product.astype(BACK)
    back_copies = exchange(back_part, back_in, back_sem)
    for c in range(helpers):
        count_part[c:c + 1, :] = far_count[1, c:c + 1, :] + named[c]
    count_copies = []
    for j in range(1, helpers):
        c = pltpu.make_async_remote_copy(
            src_ref=count_part, dst_ref=count_in.at[j - 1],
            send_sem=count_sem.at[0, j - 1], recv_sem=count_sem.at[1, j - 1],
            device_id={"help": lax.rem(h + j, helpers)}, device_id_type=MESH,
        )
        c.start()
        count_copies.append(c)
    finish(back_copies)
    back_move.wait()
    total = back_part[h].astype(F32) + far_back[1].astype(F32)
    for j in range(helpers - 1):
        total = total + back_in[j].astype(F32)
    back[h] = total.astype(FULL)
    back_copies = publish(back.at[h], back.at[h], back2_sem)
    finish(count_copies)
    queried_all = count_part[...]
    for j in range(helpers - 1):
        queried_all = queried_all + count_in[j]
    factor = jnp.zeros((1, own_points), F32)
    for c in range(helpers):
        queried = queried_all[c:c + 1, 0:1]
        one = (1.0 / width) / jnp.sqrt((queried + 1.0) * (queried + residents[c]))
        factor = jnp.where(inside[c], one, factor)
    finish(back_copies)

    full = back[...].reshape(n, width)
    points = point[...]
    if FULL == F32:
        wide = dot_halves(full, points, 1)
    else:
        wide = dot(full, points, 1, 1)
    chosen = wide[:rank]
    for c in range(1, helpers):
        chosen = jnp.where(inside[c], wide[c * rank:(c + 1) * rank], chosen)
    result = chosen * factor
    sketch[...] = result
    sketch_copy = pltpu.make_async_copy(sketch, sketch_hbm, out_sem.at[0])
    sketch_copy.start()
    rounded = result.astype(BF16).astype(F32)
    weighted = jnp.concatenate([jnp.where(m, rounded, 0.0) for m in inside], axis=0).astype(BF16)
    last_part[...] = dot(weighted, points, 1, 0).reshape(helpers, rank, width).astype(LAST)
    finish(exchange(last_part, last_in, last_sem))
    total = last_part[h].astype(F32)
    for j in range(helpers - 1):
        total = total + last_in[j].astype(F32)
    regress[...] = (total * own_scale).reshape(1, rank, width)
    regress_copy = pltpu.make_async_copy(regress, regress_hbm, out_sem.at[1])
    regress_copy.start()

    moved = 2 * (PLANE - 1) + (planes - 2) * PLANE
    pltpu.make_async_remote_copy(
        src_ref=send.at[pl.ds(0, moved)], dst_ref=recv.at[pl.ds(0, moved)],
        send_sem=row_send, recv_sem=row_recv.at[0],
        device_id={"shard": lax.rem(s + 1, groups)}, device_id_type=MESH,
    ).wait_send()
    pltpu.make_async_remote_copy(
        src_ref=tag_send.at[pl.ds(0, moved)], dst_ref=tag_recv.at[pl.ds(0, moved)],
        send_sem=tag_ssem, recv_sem=tag_rsem.at[0],
        device_id={"shard": lax.rem(s + 1, groups)}, device_id_type=MESH,
    ).wait_send()
    sketch_copy.wait()
    regress_copy.wait()


def tag_row(tags, chunk, capacity):
    part = tags.reshape(PLANE, 128).astype(BF16)
    source = (
        lax.broadcasted_iota(I32, (PLANE, chunk), 0)
        == lax.broadcasted_iota(I32, (PLANE, chunk), 1) // capacity
    ).astype(F32).astype(BF16)
    wide = dot(part, source, 0, 0)[:capacity]
    return jnp.sum(
        jnp.where(
            lax.broadcasted_iota(I32, (capacity, chunk), 0)
            == lax.rem(lax.broadcasted_iota(I32, (capacity, chunk), 1), capacity),
            wide, 0.0,
        ),
        axis=0, keepdims=True,
    )


def shards(queries, probe_group, probe_local, points, point_cluster, test_matrix):
    groups = lax.axis_size("shard")
    helpers = lax.axis_size("help")
    rows, width = queries.shape
    probes = probe_group.shape[1]
    capacity = 2 * rows * probes // groups
    own_points = points.shape[0]
    rank = test_matrix.shape[0]
    planes = groups // PLANE
    peers = helpers - 1
    slab = (helpers, rank, width)
    away = (peers, rank, width)
    DMA = pltpu.SemaphoreType.DMA
    return pl.pallas_call(
        functools.partial(kernel, planes, helpers, capacity),
        out_shape=(
            jax.ShapeDtypeStruct((rank, own_points), F32),
            jax.ShapeDtypeStruct((1, rank, width), F32),
        ),
        in_specs=[pl.BlockSpec(memory_space=pl.ANY)] * 6,
        out_specs=(pl.BlockSpec(memory_space=pl.ANY), pl.BlockSpec(memory_space=pl.ANY)),
        scratch_shapes=[
            pltpu.VMEM((probes, rows), I32),
            pltpu.VMEM((probes, rows), I32),
            pltpu.VMEM((rows, width), BF16),
            pltpu.VMEM((own_points, width), BF16),
            pltpu.VMEM(point_cluster.shape, I32),
            pltpu.VMEM((rank, own_points), BF16),
            pltpu.VMEM((groups, capacity, width), BF16),
            pltpu.VMEM((groups, capacity, width), BF16),
            pltpu.VMEM((groups, 1, 128), F32),
            pltpu.VMEM((groups, 1, 128), F32),
            pltpu.VMEM(slab, F32),
            pltpu.VMEM(away, F32),
            pltpu.VMEM(slab, F32),
            pltpu.VMEM((helpers, 128), F32),
            pltpu.VMEM((peers, helpers, 128), F32),
            pltpu.VMEM(slab, BACK),
            pltpu.VMEM(away, BACK),
            pltpu.VMEM(slab, FULL),
            pltpu.VMEM(slab, LAST),
            pltpu.VMEM(away, LAST),
            pltpu.VMEM((rank, own_points), F32),
            pltpu.VMEM((1, rank, width), F32),
            DMA((6,)),
            DMA,
            DMA((planes,)),
            DMA((2,)),
            DMA,
            DMA((planes,)),
            DMA((2, peers)),
            DMA((2, peers)),
            DMA((2, peers)),
            DMA((2, peers)),
            DMA((2, peers)),
            DMA((2, peers)),
            DMA((2,)),
            pltpu.SemaphoreType.REGULAR((planes // 2, 2)),
            pltpu.VMEM((peers, PLANE, capacity, width), BF16),
            pltpu.VMEM((peers, PLANE, 1, 128), F32),
            pltpu.VMEM((2, rank, width), BF16),
            pltpu.VMEM((2, rank, width), BF16),
            pltpu.VMEM((2, helpers, 128), F32),
            DMA((2, peers)),
            DMA((2, peers)),
            DMA((2,)),
            DMA((2,)),
            DMA((2,)),
        ],
        compiler_params=pltpu.CompilerParams(collective_id=0, has_side_effects=True),
    )(probe_group.T, probe_local.T, queries, points, point_cluster, test_matrix)


def solution(mesh):
    in_specs = (
        P(("shard", "help"), None),
        P(("shard", "help"), None),
        P(("shard", "help"), None),
        P(("shard", "help"), None),
        P("shard", None),
        P(None, ("shard", "help")),
    )
    out_specs = (P(None, ("shard", "help")), P(("shard", "help"), None, None))
    return jax.shard_map(shards, mesh=mesh, in_specs=in_specs, out_specs=out_specs, check_vma=False)
```

```python
import functools

import jax
import jax.numpy as jnp
from jax import lax
from jax.experimental import pallas as pl
from jax.experimental.pallas import tpu as pltpu
from jax.sharding import PartitionSpec as P

F32 = jnp.float32
BF16 = jnp.bfloat16
I32 = jnp.int32
MESH = pl.DeviceIdType.MESH
PLANE = 8
BACK = BF16
FULL = BF16
LAST = BF16


def dot(a, b, ca, cb):
    return lax.dot_general(a, b, (((ca,), (cb,)), ((), ())), preferred_element_type=F32)


def stack_halves(v):
    hi = v.astype(BF16)
    lo = (v - hi.astype(F32)).astype(BF16)
    return jnp.concatenate([hi, lo], axis=0)


def dot_halves(v, w, cw):
    both = dot(stack_halves(v), w, 1, cw)
    n = v.shape[0]
    return both[:n] + both[n:]


def kernel(
    planes, helpers, capacity,
    group_hbm, local_hbm, query_hbm, point_hbm, cluster_hbm, test_hbm,
    sketch_hbm, regress_hbm,
    group, local, query, point, cluster, test,
    send, recv, tag_send, tag_recv,
    lead_part, lead_in, lead, count_part, count_in,
    back_part, back_in, back, last_part, last_in, sketch, regress,
    load_sem, row_send, row_recv, own_sem, tag_ssem, tag_rsem,
    lead_sem, lead2_sem, count_sem, back_sem, back2_sem, last_sem, out_sem, round_sem,
    far_rows, far_tags, far_lead, far_back, far_count,
    share_sem, stag_sem, flead_sem, fback_sem, fcount_sem,
):
    s = lax.axis_index("shard")
    h = lax.axis_index("help")
    z = s // PLANE
    spot = lax.rem(s, PLANE)
    groups = planes * PLANE
    rows, width = query.shape
    own_points = point.shape[0]
    rank = test.shape[0]
    slots = groups * capacity
    chunk = PLANE * capacity
    pieces, _, _, part_width = back.shape
    cut = [slice(i * part_width, (i + 1) * part_width) for i in range(pieces)]

    barrier = pltpu.get_barrier_semaphore()

    column = sorted({1, planes - 1})

    def greet(j, carry):
        pl.semaphore_signal(
            barrier, inc=1, device_id={"shard": z * PLANE + lax.rem(spot + j, PLANE)},
            device_id_type=MESH,
        )
        return carry

    def call_column(ref):
        for i, d in enumerate(column):
            pl.semaphore_signal(
                ref(i), inc=1, device_id={"shard": lax.rem(s + d * PLANE, groups)},
                device_id_type=MESH,
            )

    call_column(lambda i: barrier)
    lax.fori_loop(1, PLANE, greet, 0)
    for j in range(1, helpers):
        pl.semaphore_signal(
            barrier, inc=1, device_id={"help": lax.rem(h + j, helpers)}, device_id_type=MESH
        )

    loads = []
    for i, (a, b) in enumerate(
        ((group_hbm, group), (local_hbm, local), (query_hbm, query),
         (cluster_hbm, cluster), (test_hbm, test), (point_hbm, point))
    ):
        c = pltpu.make_async_copy(a, b, load_sem.at[i])
        c.start()
        loads.append(c)

    loads[0].wait()
    loads[1].wait()
    glabel = lax.broadcasted_iota(I32, (groups, rows), 0)
    hot = [glabel == group[k:k + 1, :] for k in range(2)]
    hotf = [m.astype(F32) for m in hot]
    earlier = (
        lax.broadcasted_iota(I32, (rows, rows), 0) < lax.broadcasted_iota(I32, (rows, rows), 1)
    ).astype(F32).astype(BF16)
    first_total = jnp.sum(hotf[0], axis=1, keepdims=True)
    before = [dot(hotf[k].astype(BF16), earlier, 1, 0) for k in range(2)]
    before[1] = before[1] + first_total
    order = [jnp.sum(hotf[k] * before[k], axis=0, keepdims=True).astype(I32) for k in range(2)]
    place = [group[k:k + 1, :] * capacity + order[k] for k in range(2)]
    lane = lax.broadcasted_iota(I32, (128, rows), 0)
    tags = sum(
        dot(
            (hotf[k] * (local[k:k + 1, :] + 1).astype(F32)).astype(BF16),
            (lane == order[k]).astype(F32).astype(BF16), 1, 1,
        )
        for k in range(2)
    )
    tag_send[...] = tags.reshape(groups, 1, 128)
    opposite = planes // 2
    zo = lax.rem(z + opposite, planes)
    across = zo * PLANE + spot
    tag_recv[pl.ds(s, 1)] = tag_send[pl.ds(s, 1)]
    tag_recv[pl.ds(across, 1)] = tag_send[pl.ds(across, 1)]

    loads[2].wait()
    slot = lax.broadcasted_iota(I32, (chunk, rows), 0)
    queries = query[...]

    def pack(dz):
        zt = lax.rem(z + dz, planes)
        base = slot + zt * chunk
        pick = ((base == place[0]) | (base == place[1])).astype(F32).astype(BF16)
        packed = dot(pick, queries, 1, 0).astype(BF16)
        send[pl.ds(zt * PLANE, PLANE)] = packed.reshape(PLANE, capacity, width)

    def ship(dz):
        zt = lax.rem(z + dz, planes)
        zd = z if dz == opposite else zt
        slot_there = across if dz == opposite else s

        def tag_copy(e, carry):
            t = lax.rem(spot + e, PLANE)
            pltpu.make_async_remote_copy(
                src_ref=tag_send.at[zt * PLANE + t], dst_ref=tag_recv.at[slot_there],
                send_sem=tag_ssem, recv_sem=tag_rsem.at[dz],
                device_id={"shard": zd * PLANE + t}, device_id_type=MESH,
            ).start()
            return carry

        def row_copy(e, carry):
            t = lax.rem(spot + e, PLANE)
            pltpu.make_async_remote_copy(
                src_ref=send.at[zt * PLANE + t], dst_ref=recv.at[slot_there],
                send_sem=row_send, recv_sem=row_recv.at[dz],
                device_id={"shard": zd * PLANE + t}, device_id_type=MESH,
            ).start()
            return carry

        low = 1 if dz in (0, opposite) else 0
        lax.fori_loop(low, PLANE, tag_copy, 0)
        lax.fori_loop(low, PLANE, row_copy, 0)

    pack(0)
    pack(opposite)
    near = [d for d in column if d != opposite]
    for d in near:
        pack(d)
    pl.semaphore_wait(barrier, len(column) + PLANE - 1 + helpers - 1)
    call_column(lambda i: round_sem.at[0, i])
    ship(0)
    ship(opposite)
    own_copy = pltpu.make_async_copy(send.at[s], recv.at[s], own_sem.at[0])
    own_copy.start()
    across_copy = pltpu.make_async_copy(send.at[across], recv.at[across], own_sem.at[1])
    across_copy.start()

    def advance(far):
        for i in range(len(column)):
            pl.semaphore_wait(round_sem.at[far - 1, i], 1)
        if far < opposite:
            call_column(lambda i: round_sem.at[far, i])

    def arrived(dz, k):
        pltpu.make_async_remote_copy(
            src_ref=send.at[pl.ds(0, k)], dst_ref=recv.at[pl.ds(0, k)],
            send_sem=row_send, recv_sem=row_recv.at[dz],
            device_id={"shard": lax.rem(s + 1, groups)}, device_id_type=MESH,
        ).wait_recv()
        pltpu.make_async_remote_copy(
            src_ref=tag_send.at[pl.ds(0, k)], dst_ref=tag_recv.at[pl.ds(0, k)],
            send_sem=tag_ssem, recv_sem=tag_rsem.at[dz],
            device_id={"shard": lax.rem(s + 1, groups)}, device_id_type=MESH,
        ).wait_recv()

    advance(1)
    for d in near:
        ship(d)

    def exchange(part, landing, sem):
        copies = []
        for j in range(1, helpers):
            t = lax.rem(h + j, helpers)
            copies.append(pltpu.make_async_remote_copy(
                src_ref=part.at[t], dst_ref=landing.at[j - 1],
                send_sem=sem.at[0, j - 1], recv_sem=sem.at[1, j - 1],
                device_id={"help": t}, device_id_type=MESH,
            ))
        for c in copies:
            c.start()
        return copies

    def publish(source, landing, sem):
        copies = []
        for j in range(1, helpers):
            t = lax.rem(h + j, helpers)
            copies.append(pltpu.make_async_remote_copy(
                src_ref=source, dst_ref=landing,
                send_sem=sem.at[0, j - 1], recv_sem=sem.at[1, j - 1],
                device_id={"help": t}, device_id_type=MESH,
            ))
        for c in copies:
            c.start()
        return copies

    def finish(copies):
        for c in copies:
            c.wait()

    for i in (3, 4, 5):
        loads[i].wait()
    mine = cluster[:, pl.ds(pl.multiple_of(h * own_points, own_points), own_points)]
    inside = [mine == c for c in range(helpers)]
    omega = test[...].astype(F32)
    spread = jnp.concatenate([jnp.where(m, omega, 0.0) for m in inside], axis=0).astype(BF16)
    lead_part[...] = dot(spread, point[...], 1, 0).reshape(helpers, rank, width)
    lead_copies = exchange(lead_part, lead_in, lead_sem)

    for far in range(2, opposite + 1):
        advance(far)
        if far < opposite:
            for dz in (far, planes - far):
                pack(dz)
                if far < opposite - 1 or far == 2:
                    ship(dz)

    def to_opposite(pair, sem):
        c = pltpu.make_async_remote_copy(
            src_ref=pair.at[0], dst_ref=pair.at[1], send_sem=sem.at[0], recv_sem=sem.at[1],
            device_id={"shard": across}, device_id_type=MESH,
        )
        c.start()
        return c

    arrived(opposite, PLANE - 1)
    across_copy.wait()
    shared = []
    for j in range(1, helpers):
        for a, b, sem in ((recv, far_rows, share_sem), (tag_recv, far_tags, stag_sem)):
            c = pltpu.make_async_remote_copy(
                src_ref=a.at[pl.ds(zo * PLANE, PLANE)], dst_ref=b.at[j - 1],
                send_sem=sem.at[0, j - 1], recv_sem=sem.at[1, j - 1],
                device_id={"help": lax.rem(h + j, helpers)}, device_id_type=MESH,
            )
            c.start()
            shared.append(c)
    far_piece = tag_row(tag_recv[pl.ds(zo * PLANE, PLANE)], chunk, capacity)
    for c in range(helpers):
        far_count[0, c:c + 1, :] = jnp.broadcast_to(
            jnp.sum((far_piece == c + 1.0).astype(F32), axis=1, keepdims=True), (1, 128)
        )
    count_move = to_opposite(far_count, fcount_sem)

    finish(lead_copies)
    total = lead_part[h]
    for j in range(helpers - 1):
        total = total + lead_in[j]
    far_lead[0] = total.astype(BF16)
    lead[h] = total
    lead_move = to_opposite(far_lead, flead_sem)
    lead_copies = publish(lead.at[h], lead.at[h], lead2_sem)
    if opposite - 1 > 2:
        for dz in (opposite - 1, opposite + 1):
            ship(dz)

    everyone = cluster[...]
    residents = [
        jnp.sum((everyone == c).astype(F32), axis=1, keepdims=True) for c in range(helpers)
    ]
    own_resident = jnp.sum((everyone == h).astype(F32), axis=1, keepdims=True)
    own_scale = 1.0 / jnp.sqrt(own_resident)

    finish(lead_copies)
    halves = stack_halves(lead[...].reshape(helpers * rank, width))
    n = helpers * rank

    acc = jnp.zeros((2 * n, width), F32)
    named = [jnp.zeros((1, 1), F32) for c in range(helpers)]

    def far_product():
        lead_move.wait()
        finish(shared)
        lead_there = far_lead[1]
        label = h.astype(F32) + 1.0
        got = jnp.zeros((2 * rank, width), F32)
        for j in range(helpers):
            if j == 0:
                far_r, piece = recv[pl.ds(zo * PLANE, PLANE)], far_piece
            else:
                far_r, piece = far_rows[j - 1], tag_row(far_tags[j - 1], chunk, capacity)
            far_r = far_r.reshape(chunk, width)
            lifted = jnp.where(piece == label, dot(lead_there, far_r, 1, 1), 0.0)
            got = got + dot(stack_halves(lifted), far_r, 1, 0)
        far_back[0] = (got[:rank] + got[rank:]).astype(BF16)
        return to_opposite(far_back, fback_sem)

    back_move = None
    for dz in sorted([d for d in range(planes) if d != opposite], key=lambda d: min(d, planes - d)):
        if back_move is None and min(dz, planes - dz) == max(opposite - 1, 1):
            back_move = far_product()
        zs = lax.rem(z + planes - dz, planes)
        arrived(dz, PLANE - 1 if dz == 0 else PLANE)
        if dz == 0:
            own_copy.wait()
        rowsy = recv[pl.ds(zs * PLANE, PLANE)].reshape(chunk, width)
        both = dot(halves, rowsy, 1, 1)
        lifted = both[:n] + both[n:]
        piece = tag_row(tag_recv[pl.ds(zs * PLANE, PLANE)], chunk, capacity)
        named = [
            named[c] + jnp.sum((piece == c + 1.0).astype(F32), axis=1, keepdims=True)
            for c in range(helpers)
        ]
        lifted = jnp.concatenate(
            [jnp.where(piece == c + 1.0, lifted[c * rank:(c + 1) * rank], 0.0) for c in range(helpers)],
            axis=0,
        )
        acc = acc + dot(stack_halves(lifted), rowsy, 1, 0)
    if back_move is None:
        back_move = far_product()
    count_move.wait()
    product = acc[:n] + acc[n:]
    back_copies = []
    for i in range(pieces):
        back_part[i] = product[:, cut[i]].reshape(helpers, rank, part_width).astype(BACK)
        back_copies.append(exchange(back_part.at[i], back_in.at[i], back_sem.at[i]))
    for c in range(helpers):
        count_part[c:c + 1, :] = far_count[1, c:c + 1, :] + named[c]
    count_copies = []
    for j in range(1, helpers):
        c = pltpu.make_async_remote_copy(
            src_ref=count_part, dst_ref=count_in.at[j - 1],
            send_sem=count_sem.at[0, j - 1], recv_sem=count_sem.at[1, j - 1],
            device_id={"help": lax.rem(h + j, helpers)}, device_id_type=MESH,
        )
        c.start()
        count_copies.append(c)
    back_move.wait()
    full_copies = []
    for i in range(pieces):
        finish(back_copies[i])
        total = back_part[i, h].astype(F32) + far_back[1, :, cut[i]].astype(F32)
        for j in range(helpers - 1):
            total = total + back_in[i, j].astype(F32)
        back[i, h] = total.astype(FULL)
        full_copies.append(publish(back.at[i, h], back.at[i, h], back2_sem.at[i]))
    finish(count_copies)
    queried_all = count_part[...]
    for j in range(helpers - 1):
        queried_all = queried_all + count_in[j]
    factor = jnp.zeros((1, own_points), F32)
    for c in range(helpers):
        queried = queried_all[c:c + 1, 0:1]
        one = (1.0 / width) / jnp.sqrt((queried + 1.0) * (queried + residents[c]))
        factor = jnp.where(inside[c], one, factor)
    wide = jnp.zeros((n, own_points), F32)
    for i in range(pieces):
        finish(full_copies[i])
        full = back[i].reshape(n, part_width)
        if FULL == F32:
            wide = wide + dot_halves(full, point[:, cut[i]], 1)
        else:
            wide = wide + dot(full, point[:, cut[i]], 1, 1)
    chosen = wide[:rank]
    for c in range(1, helpers):
        chosen = jnp.where(inside[c], wide[c * rank:(c + 1) * rank], chosen)
    result = chosen * factor
    sketch[...] = result
    sketch_copy = pltpu.make_async_copy(sketch, sketch_hbm, out_sem.at[0])
    sketch_copy.start()
    rounded = result.astype(BF16).astype(F32)
    weighted = jnp.concatenate([jnp.where(m, rounded, 0.0) for m in inside], axis=0).astype(BF16)
    last_copies = []
    for i in range(pieces):
        last = dot(weighted, point[:, cut[i]], 1, 0)
        last_part[i] = last.reshape(helpers, rank, part_width).astype(LAST)
        last_copies.append(exchange(last_part.at[i], last_in.at[i], last_sem.at[i]))
    for i in range(pieces):
        finish(last_copies[i])
        total = last_part[i, h].astype(F32)
        for j in range(helpers - 1):
            total = total + last_in[i, j].astype(F32)
        regress[0, :, cut[i]] = total * own_scale
    regress_copy = pltpu.make_async_copy(regress, regress_hbm, out_sem.at[1])
    regress_copy.start()

    moved = 2 * (PLANE - 1) + (planes - 2) * PLANE
    pltpu.make_async_remote_copy(
        src_ref=send.at[pl.ds(0, moved)], dst_ref=recv.at[pl.ds(0, moved)],
        send_sem=row_send, recv_sem=row_recv.at[0],
        device_id={"shard": lax.rem(s + 1, groups)}, device_id_type=MESH,
    ).wait_send()
    pltpu.make_async_remote_copy(
        src_ref=tag_send.at[pl.ds(0, moved)], dst_ref=tag_recv.at[pl.ds(0, moved)],
        send_sem=tag_ssem, recv_sem=tag_rsem.at[0],
        device_id={"shard": lax.rem(s + 1, groups)}, device_id_type=MESH,
    ).wait_send()
    sketch_copy.wait()
    regress_copy.wait()


def tag_row(tags, chunk, capacity):
    part = tags.reshape(PLANE, 128).astype(BF16)
    source = (
        lax.broadcasted_iota(I32, (PLANE, chunk), 0)
        == lax.broadcasted_iota(I32, (PLANE, chunk), 1) // capacity
    ).astype(F32).astype(BF16)
    wide = dot(part, source, 0, 0)[:capacity]
    return jnp.sum(
        jnp.where(
            lax.broadcasted_iota(I32, (capacity, chunk), 0)
            == lax.rem(lax.broadcasted_iota(I32, (capacity, chunk), 1), capacity),
            wide, 0.0,
        ),
        axis=0, keepdims=True,
    )


def deliver(a_ref, b_ref, a_out, b_out, a_buf, b_buf, sem):
    moves = [
        (pltpu.make_async_copy(a_ref, a_buf, sem.at[0]), pltpu.make_async_copy(a_buf, a_out, sem.at[1])),
        (pltpu.make_async_copy(b_ref, b_buf, sem.at[2]), pltpu.make_async_copy(b_buf, b_out, sem.at[3])),
    ]
    for into, out in moves:
        into.start()
    for into, out in moves:
        into.wait()
        out.start()
    for into, out in moves:
        out.wait()


def shards(queries, probe_group, probe_local, points, point_cluster, test_matrix):
    groups = lax.axis_size("shard")
    helpers = lax.axis_size("help")
    rows, width = queries.shape
    probes = probe_group.shape[1]
    capacity = 2 * rows * probes // groups
    own_points = points.shape[0]
    rank = test_matrix.shape[0]
    planes = groups // PLANE
    peers = helpers - 1
    pieces = 3 if width % 384 == 0 else 1
    slab = (helpers, rank, width)
    slabs = (pieces, helpers, rank, width // pieces)
    aways = (pieces, peers, rank, width // pieces)
    away = (peers, rank, width)
    DMA = pltpu.SemaphoreType.DMA
    made = pl.pallas_call(
        functools.partial(kernel, planes, helpers, capacity),
        out_shape=(
            jax.ShapeDtypeStruct((rank, own_points), F32),
            jax.ShapeDtypeStruct((1, rank, width), F32),
        ),
        in_specs=[pl.BlockSpec(memory_space=pl.ANY)] * 6,
        out_specs=(pl.BlockSpec(memory_space=pl.ANY), pl.BlockSpec(memory_space=pl.ANY)),
        scratch_shapes=[
            pltpu.VMEM((probes, rows), I32),
            pltpu.VMEM((probes, rows), I32),
            pltpu.VMEM((rows, width), BF16),
            pltpu.VMEM((own_points, width), BF16),
            pltpu.VMEM(point_cluster.shape, I32),
            pltpu.VMEM((rank, own_points), BF16),
            pltpu.VMEM((groups, capacity, width), BF16),
            pltpu.VMEM((groups, capacity, width), BF16),
            pltpu.VMEM((groups, 1, 128), F32),
            pltpu.VMEM((groups, 1, 128), F32),
            pltpu.VMEM(slab, F32),
            pltpu.VMEM(away, F32),
            pltpu.VMEM(slab, F32),
            pltpu.VMEM((helpers, 128), F32),
            pltpu.VMEM((peers, helpers, 128), F32),
            pltpu.VMEM(slabs, BACK),
            pltpu.VMEM(aways, BACK),
            pltpu.VMEM(slabs, FULL),
            pltpu.VMEM(slabs, LAST),
            pltpu.VMEM(aways, LAST),
            pltpu.VMEM((rank, own_points), F32),
            pltpu.VMEM((1, rank, width), F32),
            DMA((6,)),
            DMA,
            DMA((planes,)),
            DMA((2,)),
            DMA,
            DMA((planes,)),
            DMA((2, peers)),
            DMA((2, peers)),
            DMA((2, peers)),
            DMA((pieces, 2, peers)),
            DMA((pieces, 2, peers)),
            DMA((pieces, 2, peers)),
            DMA((2,)),
            pltpu.SemaphoreType.REGULAR((planes // 2, 2)),
            pltpu.VMEM((peers, PLANE, capacity, width), BF16),
            pltpu.VMEM((peers, PLANE, 1, 128), F32),
            pltpu.VMEM((2, rank, width), BF16),
            pltpu.VMEM((2, rank, width), BF16),
            pltpu.VMEM((2, helpers, 128), F32),
            DMA((2, peers)),
            DMA((2, peers)),
            DMA((2,)),
            DMA((2,)),
            DMA((2,)),
        ],
        compiler_params=pltpu.CompilerParams(collective_id=0, has_side_effects=True),
    )(probe_group.T, probe_local.T, queries, points, point_cluster, test_matrix)
    sketch_shape, regress_shape = (rank, own_points), (1, rank, width)
    return pl.pallas_call(
        deliver,
        out_shape=(
            jax.ShapeDtypeStruct(sketch_shape, F32),
            jax.ShapeDtypeStruct(regress_shape, F32),
        ),
        in_specs=[pl.BlockSpec(memory_space=pl.ANY)] * 2,
        out_specs=(pl.BlockSpec(memory_space=pl.ANY), pl.BlockSpec(memory_space=pl.ANY)),
        scratch_shapes=[pltpu.VMEM(sketch_shape, F32), pltpu.VMEM(regress_shape, F32), DMA((4,))],
    )(*made)


def solution(mesh):
    in_specs = (
        P(("shard", "help"), None),
        P(("shard", "help"), None),
        P(("shard", "help"), None),
        P(("shard", "help"), None),
        P("shard", None),
        P(None, ("shard", "help")),
    )
    out_specs = (P(None, ("shard", "help")), P(("shard", "help"), None, None))
    return jax.shard_map(shards, mesh=mesh, in_specs=in_specs, out_specs=out_specs, check_vma=False)
```

```python
import functools

import jax
import jax.numpy as jnp
from jax import lax
from jax.experimental import pallas as pl
from jax.experimental.pallas import tpu as pltpu
from jax.sharding import PartitionSpec as P

F32 = jnp.float32
BF16 = jnp.bfloat16
I32 = jnp.int32
MESH = pl.DeviceIdType.MESH
PLANE = 8
BACK = BF16
FULL = BF16
LAST = BF16


def dot(a, b, ca, cb):
    return lax.dot_general(a, b, (((ca,), (cb,)), ((), ())), preferred_element_type=F32)


def stack_halves(v):
    hi = v.astype(BF16)
    lo = (v - hi.astype(F32)).astype(BF16)
    return jnp.concatenate([hi, lo], axis=0)


def dot_halves(v, w, cw):
    both = dot(stack_halves(v), w, 1, cw)
    n = v.shape[0]
    return both[:n] + both[n:]


def kernel(
    planes, helpers, capacity,
    group_hbm, local_hbm, query_hbm, point_hbm, cluster_hbm, test_hbm,
    sketch_hbm, regress_hbm,
    group, local, query, point, cluster, test,
    send, recv, tag_send, tag_recv,
    lead_part, lead_in, lead, count_part, count_in,
    back_part, back_in, back, last_part, last_in, sketch, regress,
    load_sem, row_send, row_recv, own_sem, tag_ssem, tag_rsem,
    lead_sem, lead2_sem, count_sem, back_sem, back2_sem, last_sem, out_sem, round_sem,
    far_rows, far_tags, far_lead, far_back, far_count,
    share_sem, stag_sem, flead_sem, fback_sem, fcount_sem,
):
    s = lax.axis_index("shard")
    h = lax.axis_index("help")
    z = s // PLANE
    spot = lax.rem(s, PLANE)
    groups = planes * PLANE
    rows, width = query.shape
    own_points = point.shape[0]
    rank = test.shape[0]
    slots = groups * capacity
    chunk = PLANE * capacity
    pieces, _, _, part_width = back.shape
    cut = [slice(i * part_width, (i + 1) * part_width) for i in range(pieces)]

    barrier = pltpu.get_barrier_semaphore()

    column = sorted({1, planes - 1})

    def greet(j, carry):
        pl.semaphore_signal(
            barrier, inc=1, device_id={"shard": z * PLANE + lax.rem(spot + j, PLANE)},
            device_id_type=MESH,
        )
        return carry

    def call_column(ref):
        for i, d in enumerate(column):
            pl.semaphore_signal(
                ref(i), inc=1, device_id={"shard": lax.rem(s + d * PLANE, groups)},
                device_id_type=MESH,
            )

    call_column(lambda i: barrier)
    lax.fori_loop(1, PLANE, greet, 0)
    for j in range(1, helpers):
        pl.semaphore_signal(
            barrier, inc=1, device_id={"help": lax.rem(h + j, helpers)}, device_id_type=MESH
        )

    loads = []
    for i, (a, b) in enumerate(
        ((group_hbm, group), (local_hbm, local), (query_hbm, query),
         (cluster_hbm, cluster), (test_hbm, test), (point_hbm, point))
    ):
        c = pltpu.make_async_copy(a, b, load_sem.at[i])
        c.start()
        loads.append(c)

    loads[0].wait()
    loads[1].wait()
    glabel = lax.broadcasted_iota(I32, (groups, rows), 0)
    hot = [glabel == group[k:k + 1, :] for k in range(2)]
    hotf = [m.astype(F32) for m in hot]
    earlier = (
        lax.broadcasted_iota(I32, (rows, rows), 0) < lax.broadcasted_iota(I32, (rows, rows), 1)
    ).astype(F32).astype(BF16)
    first_total = jnp.sum(hotf[0], axis=1, keepdims=True)
    before = [dot(hotf[k].astype(BF16), earlier, 1, 0) for k in range(2)]
    before[1] = before[1] + first_total
    order = [jnp.sum(hotf[k] * before[k], axis=0, keepdims=True).astype(I32) for k in range(2)]
    place = [group[k:k + 1, :] * capacity + order[k] for k in range(2)]
    lane = lax.broadcasted_iota(I32, (128, rows), 0)
    tags = sum(
        dot(
            (hotf[k] * (local[k:k + 1, :] + 1).astype(F32)).astype(BF16),
            (lane == order[k]).astype(F32).astype(BF16), 1, 1,
        )
        for k in range(2)
    )
    tag_send[...] = tags.reshape(groups, 1, 128)
    opposite = planes // 2
    zo = lax.rem(z + opposite, planes)
    across = zo * PLANE + spot
    tag_recv[pl.ds(s, 1)] = tag_send[pl.ds(s, 1)]
    tag_recv[pl.ds(across, 1)] = tag_send[pl.ds(across, 1)]

    loads[2].wait()
    slot = lax.broadcasted_iota(I32, (chunk, rows), 0)
    queries = query[...]

    def pack(dz):
        zt = lax.rem(z + dz, planes)
        base = slot + zt * chunk
        pick = ((base == place[0]) | (base == place[1])).astype(F32).astype(BF16)
        packed = dot(pick, queries, 1, 0).astype(BF16)
        send[pl.ds(zt * PLANE, PLANE)] = packed.reshape(PLANE, capacity, width)

    def ship(dz):
        zt = lax.rem(z + dz, planes)
        zd = z if dz == opposite else zt
        slot_there = across if dz == opposite else s

        def tag_copy(e, carry):
            t = lax.rem(spot + e, PLANE)
            pltpu.make_async_remote_copy(
                src_ref=tag_send.at[zt * PLANE + t], dst_ref=tag_recv.at[slot_there],
                send_sem=tag_ssem, recv_sem=tag_rsem.at[dz],
                device_id={"shard": zd * PLANE + t}, device_id_type=MESH,
            ).start()
            return carry

        def row_copy(e, carry):
            t = lax.rem(spot + e, PLANE)
            pltpu.make_async_remote_copy(
                src_ref=send.at[zt * PLANE + t], dst_ref=recv.at[slot_there],
                send_sem=row_send, recv_sem=row_recv.at[dz],
                device_id={"shard": zd * PLANE + t}, device_id_type=MESH,
            ).start()
            return carry

        low = 1 if dz in (0, opposite) else 0
        lax.fori_loop(low, PLANE, tag_copy, 0)
        lax.fori_loop(low, PLANE, row_copy, 0)

    pack(0)
    pack(opposite)
    near = [d for d in column if d != opposite]
    for d in near:
        pack(d)
    pl.semaphore_wait(barrier, len(column) + PLANE - 1 + helpers - 1)
    call_column(lambda i: round_sem.at[0, i])
    ship(0)
    ship(opposite)
    own_copy = pltpu.make_async_copy(send.at[s], recv.at[s], own_sem.at[0])
    own_copy.start()
    across_copy = pltpu.make_async_copy(send.at[across], recv.at[across], own_sem.at[1])
    across_copy.start()

    def advance(far):
        for i in range(len(column)):
            pl.semaphore_wait(round_sem.at[far - 1, i], 1)
        if far < opposite:
            call_column(lambda i: round_sem.at[far, i])

    def arrived(dz, k):
        pltpu.make_async_remote_copy(
            src_ref=send.at[pl.ds(0, k)], dst_ref=recv.at[pl.ds(0, k)],
            send_sem=row_send, recv_sem=row_recv.at[dz],
            device_id={"shard": lax.rem(s + 1, groups)}, device_id_type=MESH,
        ).wait_recv()
        pltpu.make_async_remote_copy(
            src_ref=tag_send.at[pl.ds(0, k)], dst_ref=tag_recv.at[pl.ds(0, k)],
            send_sem=tag_ssem, recv_sem=tag_rsem.at[dz],
            device_id={"shard": lax.rem(s + 1, groups)}, device_id_type=MESH,
        ).wait_recv()

    advance(1)
    for d in near:
        ship(d)

    def exchange(part, landing, sem):
        copies = []
        for j in range(1, helpers):
            t = lax.rem(h + j, helpers)
            copies.append(pltpu.make_async_remote_copy(
                src_ref=part.at[t], dst_ref=landing.at[j - 1],
                send_sem=sem.at[0, j - 1], recv_sem=sem.at[1, j - 1],
                device_id={"help": t}, device_id_type=MESH,
            ))
        for i in sorted(range(helpers - 1), key=lambda i: -min(i + 1, helpers - 1 - i)):
            copies[i].start()
        return copies

    def publish(source, landing, sem):
        copies = []
        for j in range(1, helpers):
            t = lax.rem(h + j, helpers)
            copies.append(pltpu.make_async_remote_copy(
                src_ref=source, dst_ref=landing,
                send_sem=sem.at[0, j - 1], recv_sem=sem.at[1, j - 1],
                device_id={"help": t}, device_id_type=MESH,
            ))
        for i in sorted(range(helpers - 1), key=lambda i: -min(i + 1, helpers - 1 - i)):
            copies[i].start()
        return copies

    def finish(copies):
        for c in copies:
            c.wait()

    for i in (3, 4, 5):
        loads[i].wait()
    mine = cluster[:, pl.ds(pl.multiple_of(h * own_points, own_points), own_points)]
    inside = [mine == c for c in range(helpers)]
    omega = test[...].astype(F32)
    spread = jnp.concatenate([jnp.where(m, omega, 0.0) for m in inside], axis=0).astype(BF16)
    lead_part[...] = dot(spread, point[...], 1, 0).reshape(helpers, rank, width)
    lead_copies = exchange(lead_part, lead_in, lead_sem)

    for far in range(2, opposite + 1):
        advance(far)
        if far < opposite:
            for dz in (far, planes - far):
                pack(dz)
                if far < opposite - 1 or far == 2:
                    ship(dz)

    def to_opposite(pair, sem):
        c = pltpu.make_async_remote_copy(
            src_ref=pair.at[0], dst_ref=pair.at[1], send_sem=sem.at[0], recv_sem=sem.at[1],
            device_id={"shard": across}, device_id_type=MESH,
        )
        c.start()
        return c

    arrived(opposite, PLANE - 1)
    across_copy.wait()
    shared = []
    for j in range(1, helpers):
        for a, b, sem in ((recv, far_rows, share_sem), (tag_recv, far_tags, stag_sem)):
            c = pltpu.make_async_remote_copy(
                src_ref=a.at[pl.ds(zo * PLANE, PLANE)], dst_ref=b.at[j - 1],
                send_sem=sem.at[0, j - 1], recv_sem=sem.at[1, j - 1],
                device_id={"help": lax.rem(h + j, helpers)}, device_id_type=MESH,
            )
            c.start()
            shared.append(c)
    far_piece = tag_row(tag_recv[pl.ds(zo * PLANE, PLANE)], chunk, capacity)
    for c in range(helpers):
        far_count[0, c:c + 1, :] = jnp.broadcast_to(
            jnp.sum((far_piece == c + 1.0).astype(F32), axis=1, keepdims=True), (1, 128)
        )
    count_move = to_opposite(far_count, fcount_sem)

    finish(lead_copies)
    total = lead_part[h]
    for j in range(helpers - 1):
        total = total + lead_in[j]
    far_lead[0] = total.astype(BF16)
    lead[h] = total
    lead_move = to_opposite(far_lead, flead_sem)
    lead_copies = publish(lead.at[h], lead.at[h], lead2_sem)
    if opposite - 1 > 2:
        for dz in (opposite - 1, opposite + 1):
            ship(dz)

    everyone = cluster[...]
    residents = [
        jnp.sum((everyone == c).astype(F32), axis=1, keepdims=True) for c in range(helpers)
    ]
    own_resident = jnp.sum((everyone == h).astype(F32), axis=1, keepdims=True)
    own_scale = 1.0 / jnp.sqrt(own_resident)

    finish(lead_copies)
    halves = stack_halves(lead[...].reshape(helpers * rank, width))
    n = helpers * rank

    acc = jnp.zeros((2 * n, width), F32)
    named = [jnp.zeros((1, 1), F32) for c in range(helpers)]

    def far_product():
        lead_move.wait()
        finish(shared)
        lead_there = far_lead[1]
        label = h.astype(F32) + 1.0
        got = jnp.zeros((2 * rank, width), F32)
        for j in range(helpers):
            if j == 0:
                far_r, piece = recv[pl.ds(zo * PLANE, PLANE)], far_piece
            else:
                far_r, piece = far_rows[j - 1], tag_row(far_tags[j - 1], chunk, capacity)
            far_r = far_r.reshape(chunk, width)
            lifted = jnp.where(piece == label, dot(lead_there, far_r, 1, 1), 0.0)
            got = got + dot(stack_halves(lifted), far_r, 1, 0)
        far_back[0] = (got[:rank] + got[rank:]).astype(BF16)
        return to_opposite(far_back, fback_sem)

    back_move = None
    for dz in sorted([d for d in range(planes) if d != opposite], key=lambda d: min(d, planes - d)):
        if back_move is None and min(dz, planes - dz) == 2:
            back_move = far_product()
        zs = lax.rem(z + planes - dz, planes)
        arrived(dz, PLANE - 1 if dz == 0 else PLANE)
        if dz == 0:
            own_copy.wait()
        rowsy = recv[pl.ds(zs * PLANE, PLANE)].reshape(chunk, width)
        both = dot(halves, rowsy, 1, 1)
        lifted = both[:n] + both[n:]
        piece = tag_row(tag_recv[pl.ds(zs * PLANE, PLANE)], chunk, capacity)
        named = [
            named[c] + jnp.sum((piece == c + 1.0).astype(F32), axis=1, keepdims=True)
            for c in range(helpers)
        ]
        lifted = jnp.concatenate(
            [jnp.where(piece == c + 1.0, lifted[c * rank:(c + 1) * rank], 0.0) for c in range(helpers)],
            axis=0,
        )
        acc = acc + dot(stack_halves(lifted), rowsy, 1, 0)
    if back_move is None:
        back_move = far_product()
    count_move.wait()
    product = acc[:n] + acc[n:]
    back_copies = []
    for i in range(pieces):
        back_part[i] = product[:, cut[i]].reshape(helpers, rank, part_width).astype(BACK)
        back_copies.append(exchange(back_part.at[i], back_in.at[i], back_sem.at[i]))
    for c in range(helpers):
        count_part[c:c + 1, :] = far_count[1, c:c + 1, :] + named[c]
    count_copies = []
    for j in range(1, helpers):
        c = pltpu.make_async_remote_copy(
            src_ref=count_part, dst_ref=count_in.at[j - 1],
            send_sem=count_sem.at[0, j - 1], recv_sem=count_sem.at[1, j - 1],
            device_id={"help": lax.rem(h + j, helpers)}, device_id_type=MESH,
        )
        c.start()
        count_copies.append(c)
    back_move.wait()
    full_copies = []
    for i in range(pieces):
        finish(back_copies[i])
        total = back_part[i, h].astype(F32) + far_back[1, :, cut[i]].astype(F32)
        for j in range(helpers - 1):
            total = total + back_in[i, j].astype(F32)
        back[i, h] = total.astype(FULL)
        full_copies.append(publish(back.at[i, h], back.at[i, h], back2_sem.at[i]))
    finish(count_copies)
    queried_all = count_part[...]
    for j in range(helpers - 1):
        queried_all = queried_all + count_in[j]
    factor = jnp.zeros((1, own_points), F32)
    for c in range(helpers):
        queried = queried_all[c:c + 1, 0:1]
        one = (1.0 / width) / jnp.sqrt((queried + 1.0) * (queried + residents[c]))
        factor = jnp.where(inside[c], one, factor)
    wide = jnp.zeros((n, own_points), F32)
    for i in range(pieces):
        finish(full_copies[i])
        full = back[i].reshape(n, part_width)
        if FULL == F32:
            wide = wide + dot_halves(full, point[:, cut[i]], 1)
        else:
            wide = wide + dot(full, point[:, cut[i]], 1, 1)
    chosen = wide[:rank]
    for c in range(1, helpers):
        chosen = jnp.where(inside[c], wide[c * rank:(c + 1) * rank], chosen)
    result = chosen * factor
    sketch[...] = result
    sketch_copy = pltpu.make_async_copy(sketch, sketch_hbm, out_sem.at[0])
    sketch_copy.start()
    rounded = result.astype(BF16).astype(F32)
    weighted = jnp.concatenate([jnp.where(m, rounded, 0.0) for m in inside], axis=0).astype(BF16)
    last_copies = []
    for i in range(pieces):
        last = dot(weighted, point[:, cut[i]], 1, 0)
        last_part[i] = last.reshape(helpers, rank, part_width).astype(LAST)
        last_copies.append(exchange(last_part.at[i], last_in.at[i], last_sem.at[i]))
    for i in range(pieces):
        finish(last_copies[i])
        total = last_part[i, h].astype(F32)
        for j in range(helpers - 1):
            total = total + last_in[i, j].astype(F32)
        regress[0, :, cut[i]] = total * own_scale
    regress_copy = pltpu.make_async_copy(regress, regress_hbm, out_sem.at[1])
    regress_copy.start()

    moved = 2 * (PLANE - 1) + (planes - 2) * PLANE
    pltpu.make_async_remote_copy(
        src_ref=send.at[pl.ds(0, moved)], dst_ref=recv.at[pl.ds(0, moved)],
        send_sem=row_send, recv_sem=row_recv.at[0],
        device_id={"shard": lax.rem(s + 1, groups)}, device_id_type=MESH,
    ).wait_send()
    pltpu.make_async_remote_copy(
        src_ref=tag_send.at[pl.ds(0, moved)], dst_ref=tag_recv.at[pl.ds(0, moved)],
        send_sem=tag_ssem, recv_sem=tag_rsem.at[0],
        device_id={"shard": lax.rem(s + 1, groups)}, device_id_type=MESH,
    ).wait_send()
    sketch_copy.wait()
    regress_copy.wait()


def tag_row(tags, chunk, capacity):
    part = tags.reshape(PLANE, 128).astype(BF16)
    source = (
        lax.broadcasted_iota(I32, (PLANE, chunk), 0)
        == lax.broadcasted_iota(I32, (PLANE, chunk), 1) // capacity
    ).astype(F32).astype(BF16)
    wide = dot(part, source, 0, 0)[:capacity]
    return jnp.sum(
        jnp.where(
            lax.broadcasted_iota(I32, (capacity, chunk), 0)
            == lax.rem(lax.broadcasted_iota(I32, (capacity, chunk), 1), capacity),
            wide, 0.0,
        ),
        axis=0, keepdims=True,
    )


def deliver(a_ref, b_ref, a_out, b_out, a_buf, b_buf, sem):
    moves = [
        (pltpu.make_async_copy(a_ref, a_buf, sem.at[0]), pltpu.make_async_copy(a_buf, a_out, sem.at[1])),
        (pltpu.make_async_copy(b_ref, b_buf, sem.at[2]), pltpu.make_async_copy(b_buf, b_out, sem.at[3])),
    ]
    for into, out in moves:
        into.start()
    for into, out in moves:
        into.wait()
        out.start()
    for into, out in moves:
        out.wait()


def shards(queries, probe_group, probe_local, points, point_cluster, test_matrix):
    groups = lax.axis_size("shard")
    helpers = lax.axis_size("help")
    rows, width = queries.shape
    probes = probe_group.shape[1]
    capacity = 2 * rows * probes // groups
    own_points = points.shape[0]
    rank = test_matrix.shape[0]
    planes = groups // PLANE
    peers = helpers - 1
    pieces = 3 if width % 384 == 0 else 1
    slab = (helpers, rank, width)
    slabs = (pieces, helpers, rank, width // pieces)
    aways = (pieces, peers, rank, width // pieces)
    away = (peers, rank, width)
    DMA = pltpu.SemaphoreType.DMA
    made = pl.pallas_call(
        functools.partial(kernel, planes, helpers, capacity),
        out_shape=(
            jax.ShapeDtypeStruct((rank, own_points), F32),
            jax.ShapeDtypeStruct((1, rank, width), F32),
        ),
        in_specs=[pl.BlockSpec(memory_space=pl.ANY)] * 6,
        out_specs=(pl.BlockSpec(memory_space=pl.ANY), pl.BlockSpec(memory_space=pl.ANY)),
        scratch_shapes=[
            pltpu.VMEM((probes, rows), I32),
            pltpu.VMEM((probes, rows), I32),
            pltpu.VMEM((rows, width), BF16),
            pltpu.VMEM((own_points, width), BF16),
            pltpu.VMEM(point_cluster.shape, I32),
            pltpu.VMEM((rank, own_points), BF16),
            pltpu.VMEM((groups, capacity, width), BF16),
            pltpu.VMEM((groups, capacity, width), BF16),
            pltpu.VMEM((groups, 1, 128), F32),
            pltpu.VMEM((groups, 1, 128), F32),
            pltpu.VMEM(slab, F32),
            pltpu.VMEM(away, F32),
            pltpu.VMEM(slab, F32),
            pltpu.VMEM((helpers, 128), F32),
            pltpu.VMEM((peers, helpers, 128), F32),
            pltpu.VMEM(slabs, BACK),
            pltpu.VMEM(aways, BACK),
            pltpu.VMEM(slabs, FULL),
            pltpu.VMEM(slabs, LAST),
            pltpu.VMEM(aways, LAST),
            pltpu.VMEM((rank, own_points), F32),
            pltpu.VMEM((1, rank, width), F32),
            DMA((6,)),
            DMA,
            DMA((planes,)),
            DMA((2,)),
            DMA,
            DMA((planes,)),
            DMA((2, peers)),
            DMA((2, peers)),
            DMA((2, peers)),
            DMA((pieces, 2, peers)),
            DMA((pieces, 2, peers)),
            DMA((pieces, 2, peers)),
            DMA((2,)),
            pltpu.SemaphoreType.REGULAR((planes // 2, 2)),
            pltpu.VMEM((peers, PLANE, capacity, width), BF16),
            pltpu.VMEM((peers, PLANE, 1, 128), F32),
            pltpu.VMEM((2, rank, width), BF16),
            pltpu.VMEM((2, rank, width), BF16),
            pltpu.VMEM((2, helpers, 128), F32),
            DMA((2, peers)),
            DMA((2, peers)),
            DMA((2,)),
            DMA((2,)),
            DMA((2,)),
        ],
        compiler_params=pltpu.CompilerParams(collective_id=0, has_side_effects=True),
    )(probe_group.T, probe_local.T, queries, points, point_cluster, test_matrix)
    sketch_shape, regress_shape = (rank, own_points), (1, rank, width)
    return pl.pallas_call(
        deliver,
        out_shape=(
            jax.ShapeDtypeStruct(sketch_shape, F32),
            jax.ShapeDtypeStruct(regress_shape, F32),
        ),
        in_specs=[pl.BlockSpec(memory_space=pl.ANY)] * 2,
        out_specs=(pl.BlockSpec(memory_space=pl.ANY), pl.BlockSpec(memory_space=pl.ANY)),
        scratch_shapes=[pltpu.VMEM(sketch_shape, F32), pltpu.VMEM(regress_shape, F32), DMA((4,))],
    )(*made)


def solution(mesh):
    in_specs = (
        P(("shard", "help"), None),
        P(("shard", "help"), None),
        P(("shard", "help"), None),
        P(("shard", "help"), None),
        P("shard", None),
        P(None, ("shard", "help")),
    )
    out_specs = (P(None, ("shard", "help")), P(("shard", "help"), None, None))
    return jax.shard_map(shards, mesh=mesh, in_specs=in_specs, out_specs=out_specs, check_vma=False)
```

```python
import functools

import jax
import jax.numpy as jnp
from jax import lax
from jax.experimental import pallas as pl
from jax.experimental.pallas import tpu as pltpu
from jax.sharding import PartitionSpec as P

F32 = jnp.float32
BF16 = jnp.bfloat16
I32 = jnp.int32
MESH = pl.DeviceIdType.MESH
PLANE = 8
BACK = BF16
FULL = BF16
LAST = BF16


def dot(a, b, ca, cb):
    return lax.dot_general(a, b, (((ca,), (cb,)), ((), ())), preferred_element_type=F32)


def stack_halves(v):
    hi = v.astype(BF16)
    lo = (v - hi.astype(F32)).astype(BF16)
    return jnp.concatenate([hi, lo], axis=0)


def dot_halves(v, w, cw):
    both = dot(stack_halves(v), w, 1, cw)
    n = v.shape[0]
    return both[:n] + both[n:]


def kernel(
    planes, helpers, capacity,
    group_hbm, local_hbm, query_hbm, point_hbm, cluster_hbm, test_hbm,
    sketch_hbm, regress_hbm,
    group, local, query, point, cluster, test,
    send, recv, tag_send, tag_recv,
    lead_part, lead_in, lead, count_part, count_in,
    back_part, back_in, back, last_part, last_in, sketch, regress,
    load_sem, row_send, row_recv, own_sem, tag_ssem, tag_rsem,
    lead_sem, lead2_sem, count_sem, back_sem, back2_sem, last_sem, out_sem, round_sem,
    far_rows, far_tags, far_lead, far_back, far_count,
    share_sem, stag_sem, flead_sem, fback_sem, fcount_sem,
):
    s = lax.axis_index("shard")
    h = lax.axis_index("help")
    z = s // PLANE
    spot = lax.rem(s, PLANE)
    groups = planes * PLANE
    rows, width = query.shape
    own_points = point.shape[0]
    rank = test.shape[0]
    slots = groups * capacity
    chunk = PLANE * capacity
    pieces, _, _, part_width = back.shape
    cut = [slice(i * part_width, (i + 1) * part_width) for i in range(pieces)]

    barrier = pltpu.get_barrier_semaphore()

    column = sorted({1, planes - 1})

    def greet(j, carry):
        pl.semaphore_signal(
            barrier, inc=1, device_id={"shard": z * PLANE + lax.rem(spot + j, PLANE)},
            device_id_type=MESH,
        )
        return carry

    def call_column(ref):
        for i, d in enumerate(column):
            pl.semaphore_signal(
                ref(i), inc=1, device_id={"shard": lax.rem(s + d * PLANE, groups)},
                device_id_type=MESH,
            )

    call_column(lambda i: barrier)
    lax.fori_loop(1, PLANE, greet, 0)
    for j in range(1, helpers):
        pl.semaphore_signal(
            barrier, inc=1, device_id={"help": lax.rem(h + j, helpers)}, device_id_type=MESH
        )

    loads = []
    for i, (a, b) in enumerate(
        ((group_hbm, group), (local_hbm, local), (query_hbm, query),
         (cluster_hbm, cluster), (test_hbm, test), (point_hbm, point))
    ):
        c = pltpu.make_async_copy(a, b, load_sem.at[i])
        c.start()
        loads.append(c)

    loads[0].wait()
    loads[1].wait()
    glabel = lax.broadcasted_iota(I32, (groups, rows), 0)
    hot = [glabel == group[k:k + 1, :] for k in range(2)]
    hotf = [m.astype(F32) for m in hot]
    earlier = (
        lax.broadcasted_iota(I32, (rows, rows), 0) < lax.broadcasted_iota(I32, (rows, rows), 1)
    ).astype(F32).astype(BF16)
    first_total = jnp.sum(hotf[0], axis=1, keepdims=True)
    before = [dot(hotf[k].astype(BF16), earlier, 1, 0) for k in range(2)]
    before[1] = before[1] + first_total
    order = [jnp.sum(hotf[k] * before[k], axis=0, keepdims=True).astype(I32) for k in range(2)]
    place = [group[k:k + 1, :] * capacity + order[k] for k in range(2)]
    lane = lax.broadcasted_iota(I32, (128, rows), 0)
    tags = sum(
        dot(
            (hotf[k] * (local[k:k + 1, :] + 1).astype(F32)).astype(BF16),
            (lane == order[k]).astype(F32).astype(BF16), 1, 1,
        )
        for k in range(2)
    )
    tag_send[...] = tags.reshape(groups, 1, 128)
    opposite = planes // 2
    zo = lax.rem(z + opposite, planes)
    across = zo * PLANE + spot
    tag_recv[pl.ds(s, 1)] = tag_send[pl.ds(s, 1)]
    tag_recv[pl.ds(across, 1)] = tag_send[pl.ds(across, 1)]

    loads[2].wait()
    slot = lax.broadcasted_iota(I32, (chunk, rows), 0)
    queries = query[...]

    def pack(dz):
        zt = lax.rem(z + dz, planes)
        base = slot + zt * chunk
        pick = ((base == place[0]) | (base == place[1])).astype(F32).astype(BF16)
        packed = dot(pick, queries, 1, 0).astype(BF16)
        send[pl.ds(zt * PLANE, PLANE)] = packed.reshape(PLANE, capacity, width)

    def ship(dz):
        zt = lax.rem(z + dz, planes)
        zd = z if dz == opposite else zt
        slot_there = across if dz == opposite else s

        def tag_copy(e, carry):
            t = lax.rem(spot + e, PLANE)
            pltpu.make_async_remote_copy(
                src_ref=tag_send.at[zt * PLANE + t], dst_ref=tag_recv.at[slot_there],
                send_sem=tag_ssem, recv_sem=tag_rsem.at[dz],
                device_id={"shard": zd * PLANE + t}, device_id_type=MESH,
            ).start()
            return carry

        def row_copy(e, carry):
            t = lax.rem(spot + e, PLANE)
            pltpu.make_async_remote_copy(
                src_ref=send.at[zt * PLANE + t], dst_ref=recv.at[slot_there],
                send_sem=row_send, recv_sem=row_recv.at[dz],
                device_id={"shard": zd * PLANE + t}, device_id_type=MESH,
            ).start()
            return carry

        low = 1 if dz in (0, opposite) else 0
        lax.fori_loop(low, PLANE, tag_copy, 0)
        lax.fori_loop(low, PLANE, row_copy, 0)

    pack(0)
    pack(opposite)
    near = [d for d in column if d != opposite]
    for d in near:
        pack(d)
    pl.semaphore_wait(barrier, len(column) + PLANE - 1 + helpers - 1)
    call_column(lambda i: round_sem.at[0, i])
    ship(0)
    ship(opposite)
    own_copy = pltpu.make_async_copy(send.at[s], recv.at[s], own_sem.at[0])
    own_copy.start()
    across_copy = pltpu.make_async_copy(send.at[across], recv.at[across], own_sem.at[1])
    across_copy.start()

    def advance(far):
        for i in range(len(column)):
            pl.semaphore_wait(round_sem.at[far - 1, i], 1)
        if far < opposite:
            call_column(lambda i: round_sem.at[far, i])

    def arrived(dz, k):
        pltpu.make_async_remote_copy(
            src_ref=send.at[pl.ds(0, k)], dst_ref=recv.at[pl.ds(0, k)],
            send_sem=row_send, recv_sem=row_recv.at[dz],
            device_id={"shard": lax.rem(s + 1, groups)}, device_id_type=MESH,
        ).wait_recv()
        pltpu.make_async_remote_copy(
            src_ref=tag_send.at[pl.ds(0, k)], dst_ref=tag_recv.at[pl.ds(0, k)],
            send_sem=tag_ssem, recv_sem=tag_rsem.at[dz],
            device_id={"shard": lax.rem(s + 1, groups)}, device_id_type=MESH,
        ).wait_recv()

    advance(1)
    for d in near:
        ship(d)

    if opposite >= 2:
        advance(2)
        if opposite > 2:
            for dz in (2, planes - 2):
                pack(dz)
                ship(dz)

    def exchange(part, landing, sem):
        copies = []
        for j in range(1, helpers):
            t = lax.rem(h + j, helpers)
            copies.append(pltpu.make_async_remote_copy(
                src_ref=part.at[t], dst_ref=landing.at[j - 1],
                send_sem=sem.at[0, j - 1], recv_sem=sem.at[1, j - 1],
                device_id={"help": t}, device_id_type=MESH,
            ))
        for i in sorted(range(helpers - 1), key=lambda i: -min(i + 1, helpers - 1 - i)):
            copies[i].start()
        return copies

    def publish(source, landing, sem):
        copies = []
        for j in range(1, helpers):
            t = lax.rem(h + j, helpers)
            copies.append(pltpu.make_async_remote_copy(
                src_ref=source, dst_ref=landing,
                send_sem=sem.at[0, j - 1], recv_sem=sem.at[1, j - 1],
                device_id={"help": t}, device_id_type=MESH,
            ))
        for i in sorted(range(helpers - 1), key=lambda i: -min(i + 1, helpers - 1 - i)):
            copies[i].start()
        return copies

    def finish(copies):
        for c in copies:
            c.wait()

    for i in (3, 4, 5):
        loads[i].wait()
    mine = cluster[:, pl.ds(pl.multiple_of(h * own_points, own_points), own_points)]
    inside = [mine == c for c in range(helpers)]
    omega = test[...].astype(F32)
    spread = jnp.concatenate([jnp.where(m, omega, 0.0) for m in inside], axis=0).astype(BF16)
    lead_part[...] = dot(spread, point[...], 1, 0).reshape(helpers, rank, width)
    lead_copies = exchange(lead_part, lead_in, lead_sem)

    for far in range(3, opposite + 1):
        advance(far)
        if far < opposite:
            for dz in (far, planes - far):
                pack(dz)

    def to_opposite(pair, sem):
        c = pltpu.make_async_remote_copy(
            src_ref=pair.at[0], dst_ref=pair.at[1], send_sem=sem.at[0], recv_sem=sem.at[1],
            device_id={"shard": across}, device_id_type=MESH,
        )
        c.start()
        return c

    arrived(opposite, PLANE - 1)
    across_copy.wait()
    shared = []
    for j in range(1, helpers):
        for a, b, sem in ((recv, far_rows, share_sem), (tag_recv, far_tags, stag_sem)):
            c = pltpu.make_async_remote_copy(
                src_ref=a.at[pl.ds(zo * PLANE, PLANE)], dst_ref=b.at[j - 1],
                send_sem=sem.at[0, j - 1], recv_sem=sem.at[1, j - 1],
                device_id={"help": lax.rem(h + j, helpers)}, device_id_type=MESH,
            )
            c.start()
            shared.append(c)
    far_piece = tag_row(tag_recv[pl.ds(zo * PLANE, PLANE)], chunk, capacity)
    for c in range(helpers):
        far_count[0, c:c + 1, :] = jnp.broadcast_to(
            jnp.sum((far_piece == c + 1.0).astype(F32), axis=1, keepdims=True), (1, 128)
        )
    count_move = to_opposite(far_count, fcount_sem)

    finish(lead_copies)
    total = lead_part[h]
    for j in range(helpers - 1):
        total = total + lead_in[j]
    far_lead[0] = total.astype(BF16)
    lead[h] = total
    lead_move = to_opposite(far_lead, flead_sem)
    lead_copies = publish(lead.at[h], lead.at[h], lead2_sem)
    if opposite - 1 > 2:
        for dz in (opposite - 1, opposite + 1):
            ship(dz)

    everyone = cluster[...]
    residents = [
        jnp.sum((everyone == c).astype(F32), axis=1, keepdims=True) for c in range(helpers)
    ]
    own_resident = jnp.sum((everyone == h).astype(F32), axis=1, keepdims=True)
    own_scale = 1.0 / jnp.sqrt(own_resident)

    finish(lead_copies)
    halves = stack_halves(lead[...].reshape(helpers * rank, width))
    n = helpers * rank

    acc = jnp.zeros((2 * n, width), F32)
    named = [jnp.zeros((1, 1), F32) for c in range(helpers)]

    def far_product():
        lead_move.wait()
        finish(shared)
        lead_there = far_lead[1]
        label = h.astype(F32) + 1.0
        got = jnp.zeros((2 * rank, width), F32)
        for j in range(helpers):
            if j == 0:
                far_r, piece = recv[pl.ds(zo * PLANE, PLANE)], far_piece
            else:
                far_r, piece = far_rows[j - 1], tag_row(far_tags[j - 1], chunk, capacity)
            far_r = far_r.reshape(chunk, width)
            lifted = jnp.where(piece == label, dot(lead_there, far_r, 1, 1), 0.0)
            got = got + dot(stack_halves(lifted), far_r, 1, 0)
        far_back[0] = (got[:rank] + got[rank:]).astype(BF16)
        return to_opposite(far_back, fback_sem)

    back_move = None
    waves = sorted([d for d in range(planes) if d != opposite], key=lambda d: min(d, planes - d))
    for place_in, dz in enumerate(waves):
        if place_in == len(waves) - 1:
            acc = acc[:n] + acc[n:]
        if back_move is None and min(dz, planes - dz) == 2:
            back_move = far_product()
        zs = lax.rem(z + planes - dz, planes)
        arrived(dz, PLANE - 1 if dz == 0 else PLANE)
        if dz == 0:
            own_copy.wait()
        rowsy = recv[pl.ds(zs * PLANE, PLANE)].reshape(chunk, width)
        both = dot(halves, rowsy, 1, 1)
        lifted = both[:n] + both[n:]
        piece = tag_row(tag_recv[pl.ds(zs * PLANE, PLANE)], chunk, capacity)
        named = [
            named[c] + jnp.sum((piece == c + 1.0).astype(F32), axis=1, keepdims=True)
            for c in range(helpers)
        ]
        lifted = jnp.concatenate(
            [jnp.where(piece == c + 1.0, lifted[c * rank:(c + 1) * rank], 0.0) for c in range(helpers)],
            axis=0,
        )
        halved = stack_halves(lifted)
        if place_in < len(waves) - 1:
            acc = acc + dot(halved, rowsy, 1, 0)
    if back_move is None:
        back_move = far_product()
    back_copies = []
    for i in range(pieces):
        latest = dot(halved, rowsy[:, cut[i]], 1, 0)
        product = acc[:, cut[i]] + latest[:n] + latest[n:]
        back_part[i] = product.reshape(helpers, rank, part_width).astype(BACK)
        back_copies.append(exchange(back_part.at[i], back_in.at[i], back_sem.at[i]))
    count_move.wait()
    for c in range(helpers):
        count_part[c:c + 1, :] = far_count[1, c:c + 1, :] + named[c]
    count_copies = []
    for j in range(1, helpers):
        c = pltpu.make_async_remote_copy(
            src_ref=count_part, dst_ref=count_in.at[j - 1],
            send_sem=count_sem.at[0, j - 1], recv_sem=count_sem.at[1, j - 1],
            device_id={"help": lax.rem(h + j, helpers)}, device_id_type=MESH,
        )
        c.start()
        count_copies.append(c)
    back_move.wait()
    full_copies = []
    for i in range(pieces):
        finish(back_copies[i])
        total = back_part[i, h].astype(F32) + far_back[1, :, cut[i]].astype(F32)
        for j in range(helpers - 1):
            total = total + back_in[i, j].astype(F32)
        back[i, h] = total.astype(FULL)
        full_copies.append(publish(back.at[i, h], back.at[i, h], back2_sem.at[i]))
    finish(count_copies)
    queried_all = count_part[...]
    for j in range(helpers - 1):
        queried_all = queried_all + count_in[j]
    factor = jnp.zeros((1, own_points), F32)
    for c in range(helpers):
        queried = queried_all[c:c + 1, 0:1]
        one = (1.0 / width) / jnp.sqrt((queried + 1.0) * (queried + residents[c]))
        factor = jnp.where(inside[c], one, factor)
    wide = jnp.zeros((n, own_points), F32)
    for i in range(pieces):
        finish(full_copies[i])
        full = back[i].reshape(n, part_width)
        if FULL == F32:
            wide = wide + dot_halves(full, point[:, cut[i]], 1)
        else:
            wide = wide + dot(full, point[:, cut[i]], 1, 1)
    chosen = wide[:rank]
    for c in range(1, helpers):
        chosen = jnp.where(inside[c], wide[c * rank:(c + 1) * rank], chosen)
    result = chosen * factor
    sketch[...] = result
    sketch_copy = pltpu.make_async_copy(sketch, sketch_hbm, out_sem.at[0])
    sketch_copy.start()
    rounded = result.astype(BF16).astype(F32)
    weighted = jnp.concatenate([jnp.where(m, rounded, 0.0) for m in inside], axis=0).astype(BF16)
    last_copies = []
    for i in range(pieces):
        last = dot(weighted, point[:, cut[i]], 1, 0)
        last_part[i] = last.reshape(helpers, rank, part_width).astype(LAST)
        last_copies.append(exchange(last_part.at[i], last_in.at[i], last_sem.at[i]))
    for i in range(pieces):
        finish(last_copies[i])
        total = last_part[i, h].astype(F32)
        for j in range(helpers - 1):
            total = total + last_in[i, j].astype(F32)
        regress[0, :, cut[i]] = total * own_scale
    regress_copy = pltpu.make_async_copy(regress, regress_hbm, out_sem.at[1])
    regress_copy.start()

    moved = 2 * (PLANE - 1) + (planes - 2) * PLANE
    pltpu.make_async_remote_copy(
        src_ref=send.at[pl.ds(0, moved)], dst_ref=recv.at[pl.ds(0, moved)],
        send_sem=row_send, recv_sem=row_recv.at[0],
        device_id={"shard": lax.rem(s + 1, groups)}, device_id_type=MESH,
    ).wait_send()
    pltpu.make_async_remote_copy(
        src_ref=tag_send.at[pl.ds(0, moved)], dst_ref=tag_recv.at[pl.ds(0, moved)],
        send_sem=tag_ssem, recv_sem=tag_rsem.at[0],
        device_id={"shard": lax.rem(s + 1, groups)}, device_id_type=MESH,
    ).wait_send()
    sketch_copy.wait()
    regress_copy.wait()


def tag_row(tags, chunk, capacity):
    part = tags.reshape(PLANE, 128).astype(BF16)
    source = (
        lax.broadcasted_iota(I32, (PLANE, chunk), 0)
        == lax.broadcasted_iota(I32, (PLANE, chunk), 1) // capacity
    ).astype(F32).astype(BF16)
    wide = dot(part, source, 0, 0)[:capacity]
    return jnp.sum(
        jnp.where(
            lax.broadcasted_iota(I32, (capacity, chunk), 0)
            == lax.rem(lax.broadcasted_iota(I32, (capacity, chunk), 1), capacity),
            wide, 0.0,
        ),
        axis=0, keepdims=True,
    )


def deliver(a_ref, b_ref, a_out, b_out, a_buf, b_buf, sem):
    moves = [
        (pltpu.make_async_copy(a_ref, a_buf, sem.at[0]), pltpu.make_async_copy(a_buf, a_out, sem.at[1])),
        (pltpu.make_async_copy(b_ref, b_buf, sem.at[2]), pltpu.make_async_copy(b_buf, b_out, sem.at[3])),
    ]
    for into, out in moves:
        into.start()
    for into, out in moves:
        into.wait()
        out.start()
    for into, out in moves:
        out.wait()


def shards(queries, probe_group, probe_local, points, point_cluster, test_matrix):
    groups = lax.axis_size("shard")
    helpers = lax.axis_size("help")
    rows, width = queries.shape
    probes = probe_group.shape[1]
    capacity = 2 * rows * probes // groups
    own_points = points.shape[0]
    rank = test_matrix.shape[0]
    planes = groups // PLANE
    peers = helpers - 1
    pieces = 3 if width % 384 == 0 else 1
    slab = (helpers, rank, width)
    slabs = (pieces, helpers, rank, width // pieces)
    aways = (pieces, peers, rank, width // pieces)
    away = (peers, rank, width)
    DMA = pltpu.SemaphoreType.DMA
    made = pl.pallas_call(
        functools.partial(kernel, planes, helpers, capacity),
        out_shape=(
            jax.ShapeDtypeStruct((rank, own_points), F32),
            jax.ShapeDtypeStruct((1, rank, width), F32),
        ),
        in_specs=[pl.BlockSpec(memory_space=pl.ANY)] * 6,
        out_specs=(pl.BlockSpec(memory_space=pl.ANY), pl.BlockSpec(memory_space=pl.ANY)),
        scratch_shapes=[
            pltpu.VMEM((probes, rows), I32),
            pltpu.VMEM((probes, rows), I32),
            pltpu.VMEM((rows, width), BF16),
            pltpu.VMEM((own_points, width), BF16),
            pltpu.VMEM(point_cluster.shape, I32),
            pltpu.VMEM((rank, own_points), BF16),
            pltpu.VMEM((groups, capacity, width), BF16),
            pltpu.VMEM((groups, capacity, width), BF16),
            pltpu.VMEM((groups, 1, 128), F32),
            pltpu.VMEM((groups, 1, 128), F32),
            pltpu.VMEM(slab, F32),
            pltpu.VMEM(away, F32),
            pltpu.VMEM(slab, F32),
            pltpu.VMEM((helpers, 128), F32),
            pltpu.VMEM((peers, helpers, 128), F32),
            pltpu.VMEM(slabs, BACK),
            pltpu.VMEM(aways, BACK),
            pltpu.VMEM(slabs, FULL),
            pltpu.VMEM(slabs, LAST),
            pltpu.VMEM(aways, LAST),
            pltpu.VMEM((rank, own_points), F32),
            pltpu.VMEM((1, rank, width), F32),
            DMA((6,)),
            DMA,
            DMA((planes,)),
            DMA((2,)),
            DMA,
            DMA((planes,)),
            DMA((2, peers)),
            DMA((2, peers)),
            DMA((2, peers)),
            DMA((pieces, 2, peers)),
            DMA((pieces, 2, peers)),
            DMA((pieces, 2, peers)),
            DMA((2,)),
            pltpu.SemaphoreType.REGULAR((planes // 2, 2)),
            pltpu.VMEM((peers, PLANE, capacity, width), BF16),
            pltpu.VMEM((peers, PLANE, 1, 128), F32),
            pltpu.VMEM((2, rank, width), BF16),
            pltpu.VMEM((2, rank, width), BF16),
            pltpu.VMEM((2, helpers, 128), F32),
            DMA((2, peers)),
            DMA((2, peers)),
            DMA((2,)),
            DMA((2,)),
            DMA((2,)),
        ],
        compiler_params=pltpu.CompilerParams(collective_id=0, has_side_effects=True),
    )(probe_group.T, probe_local.T, queries, points, point_cluster, test_matrix)
    sketch_shape, regress_shape = (rank, own_points), (1, rank, width)
    return pl.pallas_call(
        deliver,
        out_shape=(
            jax.ShapeDtypeStruct(sketch_shape, F32),
            jax.ShapeDtypeStruct(regress_shape, F32),
        ),
        in_specs=[pl.BlockSpec(memory_space=pl.ANY)] * 2,
        out_specs=(pl.BlockSpec(memory_space=pl.ANY), pl.BlockSpec(memory_space=pl.ANY)),
        scratch_shapes=[pltpu.VMEM(sketch_shape, F32), pltpu.VMEM(regress_shape, F32), DMA((4,))],
    )(*made)


def solution(mesh):
    in_specs = (
        P(("shard", "help"), None),
        P(("shard", "help"), None),
        P(("shard", "help"), None),
        P(("shard", "help"), None),
        P("shard", None),
        P(None, ("shard", "help")),
    )
    out_specs = (P(None, ("shard", "help")), P(("shard", "help"), None, None))
    return jax.shard_map(shards, mesh=mesh, in_specs=in_specs, out_specs=out_specs, check_vma=False)
```
